32 devices in a mesh: grp: 2 (over y), tgt: 4 (over z), shot: 4 (over x, core).
Axes of the slice: x: 2, y: 2, z: 4, core: 2. Of those that a mesh axis runs over, the one named last changes fastest.
Arguments:
- adjoint_now: float32 [8, 16, 32, 256], P(('grp', 'shot'), 'tgt'), parts along dimension 0, may hold values from -6 to 6
- adjoint_later: float32 [8, 16, 32, 256], P(('grp', 'shot'), 'tgt'), parts along dimension 0, may hold values from -6 to 6
- courant: float32 [16, 32, 256], P('tgt'), may hold values from 0.15 to 0.45
- fwd_acc: bfloat16 [8, 4, 16, 32, 256], P(('grp', 'shot'), None, 'tgt'), parts along dimension 0, may hold values from -6 to 6
- surf_dest: int32 [1024, 1], P('tgt'), may hold values from 0 to 3; in each aligned block of 256 rows (0 to 255, 256 to 511, ...) at most 128 rows name the same one
- surf_cell: int32 [1024], P('tgt'), may hold values from 0 to 32767
- surf_vals: float32 [8, 4, 1024], P(('grp', 'shot'), None, 'tgt'), parts along dimension 0, may hold values from -6 to 6
Outputs:
- adjoint_final: float32 [8, 16, 32, 256], P(('grp', 'shot'), 'tgt'), parts along dimension 0
- grad: float32 [32, 32, 256], P(('grp', 'tgt')), parts along dimension 0
The draws below stay inside these ranges and needn't reach their ends.
There are 2 independent parts, one for each index of `grp`. The reference program is written for one: setup_inputs(seed, part) draws one part's arguments, and reference() takes and returns one part's arrays. A program takes and returns all parts, laid end to end along the dimension named above; an argument that names none is the same for every part. Nothing has to cross between parts.
Inputs may be any that keep to these rules, and one draw needn't show every extreme that they name: `surf_dest`: in each owner's list of 256 entries at most 128 entries name one slab, a bound that some block reaches of them; every slab is named somewhere. `surf_cell`: several entries may name the same cell; their values add.
All inputs are finite; a program needn't handle non-finite values.
Results may differ from the reference program's by a relative error of at most 0.0003.
Values sent between devices are 32-bit elements; how exact they have to be, the bound alone decides.
No kernel may reach another device: no remote copies, remote signals or barrier semaphores. Data moves between devices by JAX's collectives and lax.ppermute only.
A program may use at most 128 MiB of HBM per device.

```python
import math
import jax
import jax.numpy as jnp
import numpy as np

CX = 4
NY = 32
NZ = 256
STEPS = 4
CAP = 128
SURF_DEV = 256
SURF_ALL = 1024
SHOTS = 4
NX = 16
CELLS_DEV = 32768
N_TGT = 4


def place_ends(drawn, own_key, smallest, high):
    longest = drawn.shape.index(max(drawn.shape))
    spots = []
    for shift in (0, 1):
        where = [jax.random.randint(jax.random.fold_in(own_key, axis), (), 0, length) for axis, length in enumerate(drawn.shape)]
        where[longest] = (where[longest] + shift) % drawn.shape[longest]
        spots.append(tuple(where))
    return drawn.at[spots[0]].set(smallest).at[spots[1]].set(high)


def steps_of(key, shape, shards, low, high):
    level, own = 1.0, jax.random.fold_in(key, 6)
    for position, shards_of in shards:
        draws = jnp.exp(jax.random.uniform(jax.random.fold_in(own, position), (shards_of,), jnp.float32, low / len(shards), high / len(shards)))
        level = level * jnp.repeat(draws, shape[position] // shards_of).reshape([-1 if axis == position else 1 for axis in range(len(shape))])
    return level


def assign_block(own_key, own, number, rows, number_of, top, limit, lean):
    sequence = jax.random.permutation(own_key, number_of)
    crowded, usual = portions_of(number_of, rows * top, limit, lean, True), portions_of(number_of, rows * top, limit, lean, False)
    places = jnp.arange(number_of)

    def named(tallies, rotation):
        used = int((tallies > 0).sum())
        fixed = max(1, used // 4)
        shifted = fixed + (places - fixed + rotation * (used - fixed)) % max(1, number_of - fixed)
        return jnp.zeros((number_of,), jnp.int32).at[sequence[jnp.where(places < fixed, places, shifted)]].set(jnp.asarray(tallies, jnp.int32))

    tallies = jnp.where(number % 4 == 0, named(crowded, number // 4), named(usual, number - number // 4 - 1))
    mixed = jax.random.permutation(jax.random.fold_in(own, 3), number_of)
    donor, receiver = mixed[0:number_of // 2 * 2:2], mixed[1:number_of // 2 * 2:2]
    room = jnp.minimum(tallies[donor] - 1, limit - tallies[receiver]) // 2
    room = jnp.where((donor == sequence[0]) | (receiver == sequence[0]) | (tallies[receiver] == 0), 0, jnp.maximum(room, 0))
    shifted = jax.random.randint(jax.random.fold_in(own, 4), (number_of // 2,), 0, 1 << 20) % (room + 1)
    tallies = tallies.at[donor].add(-shifted).at[receiver].add(shifted)
    members = jnp.searchsorted(jnp.cumsum(tallies), jnp.arange(rows * top), side="right").astype(jnp.int32)
    table = members.reshape(top, rows).T
    table = table[jax.random.permutation(jax.random.fold_in(own, 1), rows)]
    rotation = jax.random.randint(jax.random.fold_in(own, 2), (rows, 1), 0, top)
    return jnp.take_along_axis(table, (jnp.arange(top)[None, :] + rotation) % top, axis=1)


def portions_of(count, total, reach, skew, full):
    portions = [(1 << 20) // math.isqrt(grade ** skew) + 1 for grade in range(1, count + 1)]
    largest = reach if full else min(reach, max(-(-total // count), total * portions[0] // sum(portions)))
    least = 1 if total - largest >= count - 1 else 0
    holding, spare = [largest] + [least] * (count - 1), total - largest - least * (count - 1)
    while spare > 0:
        free = [i for i in range(1, count) if holding[i] < largest] or [i for i in range(1, count) if holding[i] < reach]
        pool, remaining = sum([portions[i] for i in free]), spare
        for i in free:
            more = min(reach - holding[i], max(1, remaining * portions[i] // pool), spare)
            holding[i] = holding[i] + more
            spare = spare - more
    return np.array(holding)


def centred(stream_key, extent, width, reach, cuts=(), kind=jnp.bfloat16):
    drawn = jax.random.normal(stream_key, extent, jnp.float32) * width
    if len(cuts) > 0:
        drawn = steps_of(stream_key, extent, cuts, -0.22, 0.18) * drawn
    return jnp.clip(drawn, min=-reach, max=reach).astype(kind)


def setup_inputs(seed: int = 0, part: int = 0) -> dict:
    streams_of = jax.random.split(jax.random.key(seed), 8)
    own_keys = jax.random.split(jax.random.fold_in(streams_of[7], part), 8)
    adjoint_now = centred(own_keys[0], (SHOTS, NX, NY, NZ), 1.0, 6.0, ((0, 4), (1, 4)), jnp.float32)
    adjoint_later = centred(own_keys[1], (SHOTS, NX, NY, NZ), 1.0, 6.0, ((0, 4), (1, 4)), jnp.float32)
    courant = jnp.clip(jnp.exp(math.log(0.45) - 1.0986122 * jax.random.uniform(streams_of[2], (NX, NY, NZ), jnp.float32) ** steps_of(streams_of[2], (NX, NY, NZ), ((0, 4),), -0.2, 0.2)), 0.15, 0.45)
    fwd_acc = centred(own_keys[3], (SHOTS, STEPS, NX, NY, NZ), 1.0, 6.0, ((0, 4), (2, 4)))
    surf_dest_keys = jax.random.split(jax.random.fold_in(streams_of[4], 1), SURF_ALL // SURF_DEV)
    surf_dest_turns = jax.random.permutation(jax.random.fold_in(streams_of[4], 3), SURF_ALL // SURF_DEV)
    surf_dest = jax.vmap(lambda own, number: assign_block(jax.random.fold_in(streams_of[4], 2), own, number, SURF_DEV, N_TGT, 1, CAP, 2))(surf_dest_keys, surf_dest_turns).reshape((SURF_ALL, 1))
    surf_cell = place_ends(jax.random.randint(streams_of[5], (SURF_ALL,), 0, CELLS_DEV), jax.random.fold_in(streams_of[5], 1), 0, CELLS_DEV - 1).astype(jnp.int32)
    surf_vals = centred(own_keys[6], (SHOTS, STEPS, SURF_ALL), 1.0, 6.0, ((0, 4), (2, 4)), jnp.float32)
    return {"adjoint_now": adjoint_now, "adjoint_later": adjoint_later, "courant": courant, "fwd_acc": fwd_acc, "surf_dest": surf_dest, "surf_cell": surf_cell, "surf_vals": surf_vals}


COEFFS = (-205.0 / 72.0, 8.0 / 5.0, -1.0 / 5.0, 8.0 / 315.0, -1.0 / 560.0)


def laplace(padded, cells_x, cells_y, cells_z):
    center = padded[:, 4:4 + cells_x, 4:4 + cells_y, 4:4 + cells_z]
    total = (3.0 * COEFFS[0]) * center
    for offset in range(1, 5):
        pairs = padded[:, 4 + offset:4 + offset + cells_x, 4:4 + cells_y, 4:4 + cells_z] + padded[:, 4 - offset:4 - offset + cells_x, 4:4 + cells_y, 4:4 + cells_z]
        pairs = pairs + padded[:, 4:4 + cells_x, 4 + offset:4 + offset + cells_y, 4:4 + cells_z] + padded[:, 4:4 + cells_x, 4 - offset:4 - offset + cells_y, 4:4 + cells_z]
        pairs = pairs + padded[:, 4:4 + cells_x, 4:4 + cells_y, 4 + offset:4 + offset + cells_z] + padded[:, 4:4 + cells_x, 4:4 + cells_y, 4 - offset:4 - offset + cells_z]
        total = total + COEFFS[offset] * pairs
    return total


def reference(adjoint_now, adjoint_later, courant, fwd_acc, surf_dest, surf_cell, surf_vals):
    shot_count, cells_x, cells_y, cells_z = adjoint_now.shape
    global_cells = (surf_dest[:, 0].astype(jnp.int32) * (CX * NY * NZ) + surf_cell.astype(jnp.int32)).astype(jnp.int32)
    square = courant * courant
    current = adjoint_now
    later_field = adjoint_later
    grad = jnp.zeros((cells_x, cells_y, cells_z), jnp.float32)
    for step in range(STEPS):
        padded = jnp.pad(current, ((0, 0), (4, 4), (4, 4), (4, 4)))
        inject = jnp.zeros((shot_count, cells_x * cells_y * cells_z), jnp.float32).at[:, global_cells].add(surf_vals[:, step, :])
        inject = inject.reshape(current.shape)
        fresh = 2.0 * current - later_field + square * laplace(padded, cells_x, cells_y, cells_z) + inject
        grad = grad + jnp.sum(fwd_acc[:, step].astype(jnp.float32) * fresh / courant, axis=0)
        later_field = current
        current = fresh
    return (current, grad)
```

```python
import functools

import jax
import jax.numpy as jnp
from jax import lax
from jax.experimental import pallas as pl
from jax.experimental.pallas import tpu as pltpu
from jax.sharding import PartitionSpec as P

CAP = 128
GATHER_LIMIT = 4096

COEFFS = (-205.0 / 72.0, 8.0 / 5.0, -1.0 / 5.0, 8.0 / 315.0, -1.0 / 560.0)


def swap_pairs(count, first):
    partner = list(range(count))
    for left in range(first, count - 1, 2):
        partner[left], partner[left + 1] = left + 1, left
    return list(enumerate(partner))


def neighbours(slab, axis):
    count = lax.axis_size(axis)
    here = lax.axis_index(axis)
    even = here % 2 == 0
    outer = lax.ppermute(slab, axis, swap_pairs(count, 1))
    inner = lax.ppermute(slab, axis, swap_pairs(count, 0))
    low = jnp.where(here == 0, 0.0, jnp.where(even, outer, inner))
    high = jnp.where(here == count - 1, 0.0, jnp.where(even, inner, outer))
    return low, high


def laplace(padded):
    cells_x = padded.shape[0] - 8
    cells_y = padded.shape[1] - 8
    cells_z = padded.shape[2] - 8
    center = padded[4 : 4 + cells_x, 4 : 4 + cells_y, 4 : 4 + cells_z]
    total = 3.0 * COEFFS[0] * center
    for offset in range(1, 5):
        pairs = (
            padded[4 + offset : 4 + offset + cells_x, 4 : 4 + cells_y, 4 : 4 + cells_z]
            + padded[4 - offset : 4 - offset + cells_x, 4 : 4 + cells_y, 4 : 4 + cells_z]
        )
        pairs = (
            pairs
            + padded[4 : 4 + cells_x, 4 + offset : 4 + offset + cells_y, 4 : 4 + cells_z]
            + padded[4 : 4 + cells_x, 4 - offset : 4 - offset + cells_y, 4 : 4 + cells_z]
        )
        pairs = (
            pairs
            + padded[4 : 4 + cells_x, 4 : 4 + cells_y, 4 + offset : 4 + offset + cells_z]
            + padded[4 : 4 + cells_x, 4 : 4 + cells_y, 4 - offset : 4 - offset + cells_z]
        )
        total = total + COEFFS[offset] * pairs
    return total


def gathered_entries(surf_dest, surf_cell, surf_vals):
    steps = surf_vals.shape[1]
    owners = lax.axis_size("tgt")
    count = surf_cell.shape[0]
    pad = -(2 + steps) % 8
    table = jnp.concatenate(
        [
            surf_dest.reshape(1, count).astype(jnp.float32),
            surf_cell.reshape(1, count).astype(jnp.float32),
            surf_vals[0],
            jnp.zeros((pad, count), jnp.float32),
        ],
        axis=0,
    )
    if owners * count <= GATHER_LIMIT:
        tables = [table]
        for shift in range(1, owners):
            if owners & (owners - 1) == 0:
                route = [(i, i ^ shift) for i in range(owners)]
            else:
                route = [(i, (i + shift) % owners) for i in range(owners)]
            tables.append(lax.ppermute(table, "tgt", route))
        return tables
    target = surf_dest[:, 0]
    onehot_table = (target[:, None] == jnp.arange(owners, dtype=jnp.int32)[None, :]).astype(
        jnp.int32
    )
    ranks = jnp.sum((jnp.cumsum(onehot_table, axis=0) - 1) * onehot_table, axis=1)
    position = target * CAP + ranks
    slots = jnp.full((2 + steps + pad, owners * CAP), -1.0, jnp.float32)
    slots = slots.at[:, position].set(table)
    arrived = lax.all_to_all(
        slots.reshape(-1, owners, CAP), "tgt", split_axis=1, concat_axis=1, tiled=True
    )
    flat = arrived.reshape(-1, owners * CAP)
    chunk = 1024 if owners * CAP % 1024 == 0 else CAP
    return [flat[:, i : i + chunk] for i in range(0, owners * CAP, chunk)]


def inject_kernel(steps, here_ref, *refs):
    out_ref = refs[-1]
    rows, lanes = out_ref.shape[1], out_ref.shape[2]
    here = here_ref[0].astype(jnp.float32)
    total = None
    for table_ref in refs[:-1]:
        table = table_ref[...]
        count = table.shape[1]
        slab = table[0:1]
        cell = table[1:2].astype(jnp.int32)
        row = jnp.where(slab == here, cell // lanes, -1)
        lane = cell % lanes
        in_row = lax.broadcasted_iota(jnp.int32, (rows, count), 0) == row
        in_lane = lax.broadcasted_iota(jnp.int32, (lanes, count), 0) == lane
        spread = jnp.where(in_lane, 1.0, 0.0).astype(jnp.bfloat16)
        parts = []
        for step in range(steps):
            rest = table[2 + step : 3 + step]
            for _ in range(3):
                part = rest.astype(jnp.bfloat16).astype(jnp.float32)
                rest = rest - part
                parts.append(jnp.where(in_row, part, 0.0).astype(jnp.bfloat16))
        product = lax.dot_general(
            jnp.concatenate(parts, axis=0),
            spread,
            (((1,), (1,)), ((), ())),
            preferred_element_type=jnp.float32,
        )
        total = product if total is None else total + product
    for step in range(steps):
        first = 3 * step * rows
        out_ref[step] = (
            total[first : first + rows]
            + total[first + rows : first + 2 * rows]
            + total[first + 2 * rows : first + 3 * rows]
        )


def injection(tables, steps, rows, lanes):
    here = lax.axis_index("tgt").reshape(1)
    return pl.pallas_call(
        functools.partial(inject_kernel, steps),
        out_shape=jax.ShapeDtypeStruct((steps, rows, lanes), jnp.float32),
        in_specs=[pl.BlockSpec(memory_space=pltpu.SMEM)]
        + [pl.BlockSpec(memory_space=pltpu.VMEM)] * len(tables),
        out_specs=pl.BlockSpec(memory_space=pltpu.VMEM),
        cost_estimate=pl.CostEstimate(
            flops=6 * steps * rows * lanes * sum(t.shape[1] for t in tables),
            bytes_accessed=4 * steps * rows * lanes,
            transcendentals=0,
        ),
    )(here, *tables)


def sum_over(value, axis):
    count = lax.axis_size(axis)
    if count & (count - 1):
        return lax.psum(value, axis)
    distance = 1
    while distance < count:
        value = value + lax.ppermute(value, axis, [(i, i ^ distance) for i in range(count)])
        distance *= 2
    return value


def on_device(adjoint_now, adjoint_later, courant, fwd_acc, surf_dest, surf_cell, surf_vals):
    current = adjoint_now[0]
    later_field = adjoint_later[0]
    grid_shape = current.shape
    steps = fwd_acc.shape[1]
    tables = gathered_entries(surf_dest, surf_cell, surf_vals)
    inject = injection(tables, steps, grid_shape[0] * grid_shape[1], grid_shape[2])
    grad_total = jnp.zeros(grid_shape, jnp.float32)
    square = courant * courant
    for step in range(steps):
        low, high = neighbours(current, "tgt")
        padded = jnp.concatenate([low, current, high], axis=0)
        padded = jnp.pad(padded, ((0, 0), (4, 4), (4, 4)))
        fresh = (
            2.0 * current
            - later_field
            + square * laplace(padded)
            + inject[step].reshape(grid_shape)
        )
        grad_total = grad_total + fwd_acc[0, step].astype(jnp.float32) * fresh / courant
        later_field = current
        current = fresh
    return (current[None], sum_over(grad_total, "shot"))


def solution(mesh):
    in_specs = (
        P(("grp", "shot"), "tgt", None, None),
        P(("grp", "shot"), "tgt", None, None),
        P("tgt", None, None),
        P(("grp", "shot"), None, "tgt", None, None),
        P("tgt", None),
        P("tgt"),
        P(("grp", "shot"), None, "tgt"),
    )
    out_specs = (P(("grp", "shot"), "tgt", None, None), P(("grp", "tgt"), None, None))
    return jax.shard_map(
        on_device, mesh=mesh, in_specs=in_specs, out_specs=out_specs, check_vma=False
    )
```

```python
import functools

import jax
import jax.numpy as jnp
from jax import lax
from jax.experimental import pallas as pl
from jax.experimental.pallas import tpu as pltpu
from jax.sharding import PartitionSpec as P

CAP = 128
GATHER_LIMIT = 4096
REACH = 4
PIECES = 3

COEFFS = (-205.0 / 72.0, 8.0 / 5.0, -1.0 / 5.0, 8.0 / 315.0, -1.0 / 560.0)


def on_chip(kernel, outs, *args, flops=0):
    scalar = [a.dtype == jnp.int32 and a.ndim == 1 for a in args]
    results = pl.pallas_call(
        kernel,
        out_shape=[pltpu.VMEM(shape, jnp.float32) for shape in outs],
        in_specs=[
            pl.BlockSpec(memory_space=pltpu.SMEM if s else pltpu.VMEM) for s in scalar
        ],
        out_specs=[pl.BlockSpec(memory_space=pltpu.VMEM) for _ in outs],
        cost_estimate=pl.CostEstimate(
            flops=flops,
            bytes_accessed=sum(a.size * a.dtype.itemsize for a in args),
            transcendentals=0,
        ),
    )(
        *[
            a if s else pltpu.with_memory_space_constraint(a, pltpu.VMEM)
            for a, s in zip(args, scalar)
        ]
    )
    return list(results)


def swap_pairs(count, first):
    partner = list(range(count))
    for left in range(first, count - 1, 2):
        partner[left], partner[left + 1] = left + 1, left
    return list(enumerate(partner))


def exchange(slab):
    count = lax.axis_size("tgt")
    outer = lax.ppermute(slab, "tgt", swap_pairs(count, 1))
    inner = lax.ppermute(slab, "tgt", swap_pairs(count, 0))
    return inner, outer


def gathered_entries(surf_dest, surf_cell, surf_vals):
    steps = surf_vals.shape[1]
    owners = lax.axis_size("tgt")
    count = surf_cell.shape[0]
    pad = -(2 + steps) % 8
    table = jnp.concatenate(
        [
            surf_dest.reshape(1, count).astype(jnp.float32),
            surf_cell.reshape(1, count).astype(jnp.float32),
            surf_vals[0],
            jnp.zeros((pad, count), jnp.float32),
        ],
        axis=0,
    )
    if owners * count <= GATHER_LIMIT:
        tables = [table]
        for shift in range(1, owners):
            if owners & (owners - 1) == 0:
                route = [(i, i ^ shift) for i in range(owners)]
            else:
                route = [(i, (i + shift) % owners) for i in range(owners)]
            tables.append(lax.ppermute(table, "tgt", route))
        return tables, True
    target = surf_dest[:, 0]
    onehot_table = (target[:, None] == jnp.arange(owners, dtype=jnp.int32)[None, :]).astype(
        jnp.int32
    )
    ranks = jnp.sum((jnp.cumsum(onehot_table, axis=0) - 1) * onehot_table, axis=1)
    position = target * CAP + ranks
    slots = jnp.full((table.shape[0], owners * CAP), -1.0, jnp.float32)
    slots = slots.at[:, position].set(table)
    arrived = lax.all_to_all(
        slots.reshape(-1, owners, CAP), "tgt", split_axis=1, concat_axis=1, tiled=True
    )
    flat = arrived.reshape(-1, owners * CAP)
    chunk = 1024 if owners * CAP % 1024 == 0 else CAP
    return [flat[:, i : i + chunk] for i in range(0, owners * CAP, chunk)], False


def inject_kernel(steps, table_count, with_halo, here_ref, *refs):
    table_refs, out_refs = refs[:table_count], refs[table_count:]
    planes, cells_y, lanes = out_refs[0].shape
    rows = planes * cells_y
    here = here_ref[0].astype(jnp.float32)
    left, right = [], []
    for table_ref in table_refs:
        table = table_ref[...]
        count = table.shape[1]
        slab = table[0:1]
        cell = table[1:2].astype(jnp.int32)
        row, lane = cell // lanes, cell % lanes
        in_lane = lax.broadcasted_iota(jnp.int32, (lanes, count), 0) == lane
        spread = jnp.where(in_lane, 1.0, 0.0).astype(jnp.bfloat16)
        each_row = lax.broadcasted_iota(jnp.int32, (rows, count), 0)
        in_row = [each_row == jnp.where(slab == here, row, -1)]
        if with_halo:
            in_row.append(each_row == jnp.where(slab == here - 1.0, row, -1))
            in_row.append(each_row == jnp.where(slab == here + 1.0, row, -1))
        rest = [table[2 + step : 3 + step] for step in range(steps)]
        for _ in range(PIECES):
            part = [r.astype(jnp.bfloat16).astype(jnp.float32) for r in rest]
            rest = [r - p for r, p in zip(rest, part)]
            picks = [(in_row[0], p) for p in part] + [(m, part[0]) for m in in_row[1:]]
            left.append(
                jnp.concatenate(
                    [jnp.where(m, p, 0.0).astype(jnp.bfloat16) for m, p in picks], axis=0
                )
            )
            right.append(spread)
    total = lax.dot_general(
        jnp.concatenate(left, axis=1),
        jnp.concatenate(right, axis=1),
        (((1,), (1,)), ((), ())),
        preferred_element_type=jnp.float32,
    )
    for i, out_ref in enumerate(out_refs):
        out_ref[...] = total[i * rows : (i + 1) * rows].reshape(out_ref.shape)


def injection(here, tables, steps, grid_shape, with_halo):
    outs = [grid_shape] * (steps + 2 * with_halo)
    entries = sum(t.shape[1] for t in tables)
    cells = grid_shape[0] * grid_shape[1] * grid_shape[2]
    return on_chip(
        functools.partial(inject_kernel, steps, len(tables), with_halo),
        outs,
        here,
        *tables,
        flops=2 * PIECES * len(outs) * cells * entries,
    )


def plane_stencil(plane):
    cells_y, lanes = plane.shape
    at_y = lax.broadcasted_iota(jnp.int32, plane.shape, 0)
    at_z = lax.broadcasted_iota(jnp.int32, plane.shape, 1)
    total = 3.0 * COEFFS[0] * plane
    for k in range(1, REACH + 1):
        pairs = (
            jnp.where(at_y >= k, pltpu.roll(plane, k, 0), 0.0)
            + jnp.where(at_y < cells_y - k, pltpu.roll(plane, cells_y - k, 0), 0.0)
            + jnp.where(at_z >= k, pltpu.roll(plane, k, 1), 0.0)
            + jnp.where(at_z < lanes - k, pltpu.roll(plane, lanes - k, 1), 0.0)
        )
        total = total + COEFFS[k] * pairs
    return total


def own_kernel(step, has_inject, fix_inject, last, *refs):
    refs = list(refs)
    current_ref, later_ref, courant_ref = refs[:3]
    refs = refs[3:]
    inject_ref = refs.pop(0) if has_inject else None
    fix_ref = refs.pop(0) if fix_inject else None
    fwd_ref = refs.pop(0) if step else None
    grad_in_ref = refs.pop(0) if step > 1 else None
    part_ref = refs.pop(0)
    fixed_ref = refs.pop(0) if fix_inject else None
    grad_ref = refs.pop(0) if step else None
    weight_ref = refs.pop(0) if last else None
    planes = current_ref.shape[0]
    current = [current_ref[p] for p in range(planes)]
    if fix_inject:
        current = [current[p] + fix_ref[p] for p in range(planes)]
        for p in range(planes):
            fixed_ref[p] = current[p]
    for p in range(planes):
        total = plane_stencil(current[p])
        for k in range(1, REACH + 1):
            for q in (p - k, p + k):
                if 0 <= q < planes:
                    total = total + COEFFS[k] * current[q]
        courant = courant_ref[p]
        part = 2.0 * current[p] - later_ref[p] + courant * courant * total
        if has_inject:
            part = part + inject_ref[p]
        part_ref[p] = part
        if step:
            grad = fwd_ref[step - 1, p].astype(jnp.float32) * current[p]
            if step > 1:
                grad = grad + grad_in_ref[p]
            if last:
                inverse = 1.0 / courant
                grad = grad * inverse
                weight_ref[p] = fwd_ref[step, p].astype(jnp.float32) * inverse
            grad_ref[p] = grad


def halo_kernel(slabs, fix_inject, last, here_ref, *refs):
    refs = list(refs)
    inner_ref, outer_ref, part_ref, courant_ref = refs[:4]
    refs = refs[4:]
    fix_refs = (refs.pop(0), refs.pop(0)) if fix_inject else None
    weight_ref, grad_in_ref = (refs.pop(0), refs.pop(0)) if last else (None, None)
    fresh_ref = refs.pop(0)
    grad_ref = refs.pop(0) if last else None
    here = here_ref[0]
    even = here % 2 == 0
    planes = inner_ref.shape[0]
    low, high = {}, {}
    for p in range(planes - REACH, planes):
        plane = jnp.where(even, outer_ref[p], inner_ref[p])
        if fix_inject:
            plane = plane + fix_refs[0][p]
        low[p - planes] = jnp.where(here == 0, 0.0, plane)
    for p in range(REACH):
        plane = jnp.where(even, inner_ref[p], outer_ref[p])
        if fix_inject:
            plane = plane + fix_refs[1][p]
        high[p + planes] = jnp.where(here == slabs - 1, 0.0, plane)
    for p in range(planes):
        terms = []
        for k in range(1, REACH + 1):
            if p - k < 0:
                terms.append(COEFFS[k] * low[p - k])
            if p + k >= planes:
                terms.append(COEFFS[k] * high[p + k])
        courant = courant_ref[p]
        fresh = part_ref[p] + courant * courant * sum(terms[1:], terms[0])
        fresh_ref[p] = fresh
        if last:
            grad_ref[p] = grad_in_ref[p] + weight_ref[p] * fresh


def sum_over(value, axis):
    count = lax.axis_size(axis)
    if count & (count - 1):
        return lax.psum(value, axis)
    distance = 1
    while distance < count:
        value = value + lax.ppermute(value, axis, [(i, i ^ distance) for i in range(count)])
        distance *= 2
    return value


def on_device(adjoint_now, adjoint_later, courant, fwd_acc, surf_dest, surf_cell, surf_vals):
    current = adjoint_now[0]
    later_field = adjoint_later[0]
    fwd = fwd_acc[0]
    shape = current.shape
    steps = fwd.shape[0]
    slabs = lax.axis_size("tgt")
    here = lax.axis_index("tgt").reshape(1)
    tables, everywhere = gathered_entries(surf_dest, surf_cell, surf_vals)
    inject = injection(here, tables, steps, shape, everywhere)
    grad = None
    for step in range(steps):
        last = step == steps - 1
        received = exchange(current)
        fix = everywhere and step == 1
        has_inject = step > 0 or not everywhere
        args, outs = [current, later_field, courant], [shape]
        if has_inject:
            args.append(inject[step])
        if fix:
            args.append(inject[0])
            outs.append(shape)
        if step:
            args.append(fwd)
            outs.append(shape)
        if step > 1:
            args.append(grad)
        if last:
            outs.append(shape)
        results = on_chip(
            functools.partial(own_kernel, step, has_inject, fix, last),
            outs,
            *args,
            flops=40 * current.size,
        )
        part = results.pop(0)
        if fix:
            current = results.pop(0)
        if step:
            grad = results.pop(0)
        args, outs = [here, *received, part, courant], [shape]
        if fix:
            args += inject[steps:]
        if last:
            args += [results.pop(0), grad]
            outs.append(shape)
        results = on_chip(
            functools.partial(halo_kernel, slabs, fix, last), outs, *args, flops=10 * current.size
        )
        later_field, current = current, results[0]
        if last:
            grad = results[1]
    return (current[None], sum_over(grad, "shot"))


def solution(mesh):
    in_specs = (
        P(("grp", "shot"), "tgt", None, None),
        P(("grp", "shot"), "tgt", None, None),
        P("tgt", None, None),
        P(("grp", "shot"), None, "tgt", None, None),
        P("tgt", None),
        P("tgt"),
        P(("grp", "shot"), None, "tgt"),
    )
    out_specs = (P(("grp", "shot"), "tgt", None, None), P(("grp", "tgt"), None, None))
    return jax.shard_map(
        on_device, mesh=mesh, in_specs=in_specs, out_specs=out_specs, check_vma=False
    )
```

```python
import functools

import jax
import jax.numpy as jnp
from jax import lax
from jax.experimental import pallas as pl
from jax.experimental.pallas import tpu as pltpu
from jax.sharding import PartitionSpec as P

CAP = 128
GATHER_LIMIT = 4096
REACH = 4
PIECES = 3

COEFFS = (-205.0 / 72.0, 8.0 / 5.0, -1.0 / 5.0, 8.0 / 315.0, -1.0 / 560.0)


def on_chip(kernel, outs, *args, flops=0, scratch=(), in_hbm=()):
    spaces = [pltpu.SMEM if a.ndim == 1 else pltpu.VMEM for a in args]
    for i in in_hbm:
        spaces[i] = pltpu.HBM
    results = pl.pallas_call(
        kernel,
        out_shape=[pltpu.VMEM(shape, dtype) for shape, dtype in outs],
        in_specs=[pl.BlockSpec(memory_space=s) for s in spaces],
        out_specs=[pl.BlockSpec(memory_space=pltpu.VMEM) for _ in outs],
        scratch_shapes=list(scratch),
        cost_estimate=pl.CostEstimate(
            flops=flops,
            bytes_accessed=sum(a.size * a.dtype.itemsize for a in args),
            transcendentals=0,
        ),
    )(
        *[
            a if s is pltpu.SMEM else pltpu.with_memory_space_constraint(a, s)
            for a, s in zip(args, spaces)
        ]
    )
    return list(results)


def swap_pairs(count, first):
    partner = list(range(count))
    for left in range(first, count - 1, 2):
        partner[left], partner[left + 1] = left + 1, left
    return list(enumerate(partner))


def exchange(to_inner, to_outer):
    count = lax.axis_size("tgt")
    outer = lax.ppermute(to_outer, "tgt", swap_pairs(count, 1))
    inner = lax.ppermute(to_inner, "tgt", swap_pairs(count, 0))
    return inner, outer


def slotted_tables(table, surf_dest, owners):
    target = surf_dest[:, 0]
    onehot_table = (target[:, None] == jnp.arange(owners, dtype=jnp.int32)[None, :]).astype(
        jnp.int32
    )
    ranks = jnp.sum((jnp.cumsum(onehot_table, axis=0) - 1) * onehot_table, axis=1)
    position = target * CAP + ranks
    slots = jnp.full((table.shape[0], owners * CAP), -1.0, jnp.float32)
    slots = slots.at[:, position].set(table)
    arrived = lax.all_to_all(
        slots.reshape(-1, owners, CAP), "tgt", split_axis=1, concat_axis=1, tiled=True
    )
    flat = arrived.reshape(-1, owners * CAP)
    chunk = 1024 if owners * CAP % 1024 == 0 else CAP
    return [flat[:, i : i + chunk] for i in range(0, owners * CAP, chunk)]


def inject_kernel(steps, first_rows, with_halo, here_ref, *refs):
    table_refs, out_refs = refs[: len(first_rows)], refs[len(first_rows) :]
    rows, lanes = out_refs[0].shape
    here = here_ref[0].astype(jnp.float32)
    left, right = [], []
    for table_ref, firsts in zip(table_refs, first_rows):
        for first in firsts:
            table = table_ref[first : first + 2 + steps]
            count = table.shape[1]
            slab = table[0:1]
            cell = table[1:2].astype(jnp.int32)
            row, lane = cell // lanes, cell % lanes
            in_lane = lax.broadcasted_iota(jnp.int32, (lanes, count), 0) == lane
            spread = jnp.where(in_lane, 1.0, 0.0).astype(jnp.bfloat16)
            each_row = lax.broadcasted_iota(jnp.int32, (rows, count), 0)
            in_row = [each_row == jnp.where(slab == here, row, -1)]
            if with_halo:
                in_row.append(each_row == jnp.where(slab == here - 1.0, row, -1))
                in_row.append(each_row == jnp.where(slab == here + 1.0, row, -1))
            rest = [table[2 + step : 3 + step] for step in range(steps)]
            for _ in range(PIECES):
                part = [r.astype(jnp.bfloat16).astype(jnp.float32) for r in rest]
                rest = [r - p for r, p in zip(rest, part)]
                picks = [(in_row[0], p) for p in part] + [(m, part[0]) for m in in_row[1:]]
                left.append(
                    jnp.concatenate(
                        [jnp.where(m, p, 0.0).astype(jnp.bfloat16) for m, p in picks], axis=0
                    )
                )
                right.append(spread)
    total = lax.dot_general(
        jnp.concatenate(left, axis=1),
        jnp.concatenate(right, axis=1),
        (((1,), (1,)), ((), ())),
        preferred_element_type=jnp.float32,
    )
    for i, out_ref in enumerate(out_refs):
        out_ref[...] = total[i * rows : (i + 1) * rows]


def injection(here, tables, first_rows, steps, shape, with_halo):
    count = steps + 2 * with_halo
    entries = sum(t.shape[1] * len(f) for t, f in zip(tables, first_rows))
    return on_chip(
        functools.partial(inject_kernel, steps, first_rows, with_halo),
        [(shape, jnp.float32)] * count,
        here,
        *tables,
        flops=2 * PIECES * count * shape[0] * shape[1] * entries,
    )


def plane_stencil(plane):
    cells_y, lanes = plane.shape
    at_y = lax.broadcasted_iota(jnp.int32, plane.shape, 0)
    at_z = lax.broadcasted_iota(jnp.int32, plane.shape, 1)
    total = 3.0 * COEFFS[0] * plane
    for k in range(1, REACH + 1):
        pairs = (
            jnp.where(at_y >= k, pltpu.roll(plane, k, 0), 0.0)
            + jnp.where(at_y < cells_y - k, pltpu.roll(plane, cells_y - k, 0), 0.0)
            + jnp.where(at_z >= k, pltpu.roll(plane, k, 1), 0.0)
            + jnp.where(at_z < lanes - k, pltpu.roll(plane, lanes - k, 1), 0.0)
        )
        total = total + COEFFS[k] * pairs
    return total


def own_part(current, p, later, courant):
    total = plane_stencil(current[p])
    for k in range(1, REACH + 1):
        for q in (p - k, p + k):
            if 0 <= q < len(current):
                total = total + COEFFS[k] * current[q]
    return 2.0 * current[p] - later + courant * courant * total


def first_kernel(planes, table_rows, *refs):
    refs = list(refs)
    now_hbm, later_hbm, courant_hbm, fwd_hbm, dest_hbm, cell_hbm, vals_hbm = refs[:7]
    part_ref, table_ref, now_ref, courant_ref, fwd_ref = refs[7:12]
    later_ref, dest_ref, cell_ref, vals_ref, sems = refs[12:]
    pairs = [
        (dest_hbm, dest_ref),
        (cell_hbm, cell_ref),
        (vals_hbm, vals_ref),
        (now_hbm, now_ref),
        (later_hbm, later_ref),
        (courant_hbm, courant_ref),
        (fwd_hbm, fwd_ref),
    ]
    copies = [pltpu.make_async_copy(a, b, sems.at[i]) for i, (a, b) in enumerate(pairs)]
    for copy in copies:
        copy.start()
    for copy in copies[:3]:
        copy.wait()
    table_ref[...] = jnp.zeros_like(table_ref)
    table_ref[0:1] = dest_ref[...].astype(jnp.float32)
    table_ref[1:2] = cell_ref[...].astype(jnp.float32)
    table_ref[2 : 2 + vals_ref.shape[0]] = vals_ref[...]
    for copy in copies[3:6]:
        copy.wait()
    cells_y = now_ref.shape[0] // planes
    at = [slice(p * cells_y, (p + 1) * cells_y) for p in range(planes)]
    current = [now_ref[s] for s in at]
    for p, s in enumerate(at):
        part_ref[s] = own_part(current, p, later_ref[s], courant_ref[s])
    copies[6].wait()


def own_kernel(planes, step, fix_inject, last, *refs):
    refs = list(refs)
    current_ref, later_ref, courant_ref, fwd_ref, inject_ref = refs[:5]
    refs = refs[5:]
    fix_ref = refs.pop(0) if fix_inject else None
    grad_in_ref = refs.pop(0) if step > 1 else None
    part_ref = refs.pop(0)
    grad_ref = refs.pop(0)
    fixed_ref = refs.pop(0) if fix_inject else None
    weight_ref = refs.pop(0) if last else None
    cells_y = current_ref.shape[0] // planes
    at = [slice(p * cells_y, (p + 1) * cells_y) for p in range(planes)]
    current = [current_ref[s] for s in at]
    if fix_inject:
        current = [c + fix_ref[s] for c, s in zip(current, at)]
        for c, s in zip(current, at):
            fixed_ref[s] = c
    for p, s in enumerate(at):
        courant = courant_ref[s]
        part_ref[s] = own_part(current, p, later_ref[s], courant) + inject_ref[s]
        grad = fwd_ref[step - 1, s].astype(jnp.float32) * current[p]
        if step > 1:
            grad = grad + grad_in_ref[s]
        if last:
            inverse = 1.0 / courant
            grad = grad * inverse
            weight_ref[s] = fwd_ref[step, s].astype(jnp.float32) * inverse
        grad_ref[s] = grad


def halo_kernel(planes, slabs, fix_inject, last, tables, here_ref, *refs):
    refs = list(refs)
    inner_ref, outer_ref, part_ref, courant_ref = refs[:4]
    refs = refs[4:]
    fix_refs = (refs.pop(0), refs.pop(0)) if fix_inject else None
    weight_ref, grad_in_ref = (refs.pop(0), refs.pop(0)) if last else (None, None)
    table_refs = [refs.pop(0) for _ in range(tables)]
    fresh_ref = refs.pop(0)
    other_ref = refs.pop(0) if last or tables else None
    here = here_ref[0]
    even = here % 2 == 0
    rows = part_ref.shape[0]
    cells_y = rows // planes
    at = [slice(p * cells_y, (p + 1) * cells_y) for p in range(planes)]
    low, high = {}, {}
    for p in range(planes - REACH, planes):
        plane = jnp.where(even, outer_ref[at[p]], inner_ref[at[p]])
        if fix_inject:
            plane = plane + fix_refs[0][at[p]]
        low[p - planes] = jnp.where(here == 0, 0.0, plane)
    for p in range(REACH):
        plane = jnp.where(even, inner_ref[at[p]], outer_ref[at[p]])
        if fix_inject:
            plane = plane + fix_refs[1][at[p]]
        high[p + planes] = jnp.where(here == slabs - 1, 0.0, plane)
    for p, s in enumerate(at):
        terms = []
        for k in range(1, REACH + 1):
            if p - k < 0:
                terms.append(COEFFS[k] * low[p - k])
            if p + k >= planes:
                terms.append(COEFFS[k] * high[p + k])
        courant = courant_ref[s]
        fresh = part_ref[s] + courant * courant * sum(terms[1:], terms[0])
        fresh_ref[s] = fresh
        if last:
            other_ref[s] = grad_in_ref[s] + weight_ref[s] * fresh
        if tables:
            other_ref[s] = fresh
    for i, table_ref in enumerate(table_refs):
        first = rows + i * table_ref.shape[0]
        other_ref[first : first + table_ref.shape[0]] = table_ref[...]


def sum_over(value, axis):
    count = lax.axis_size(axis)
    if count & (count - 1):
        return lax.psum(value, axis)
    distance = 1
    while distance < count:
        value = value + lax.ppermute(value, axis, [(i, i ^ distance) for i in range(count)])
        distance *= 2
    return value


def on_device(adjoint_now, adjoint_later, courant, fwd_acc, surf_dest, surf_cell, surf_vals):
    planes, cells_y, lanes = courant.shape
    steps = fwd_acc.shape[1]
    rows = planes * cells_y
    shape = (rows, lanes)
    entries = surf_cell.shape[0]
    slabs = lax.axis_size("tgt")
    here = lax.axis_index("tgt").reshape(1)
    now = adjoint_now.reshape(shape)
    table_rows = -(-(2 + steps) // 8) * 8
    everywhere = (
        slabs & (slabs - 1) == 0 and slabs * entries <= GATHER_LIMIT and entries == lanes
    )

    received = exchange(now, now)
    f32 = jnp.float32
    part, table, current, courant_here, fwd = on_chip(
        functools.partial(first_kernel, planes, table_rows),
        [
            (shape, f32),
            ((table_rows, entries), f32),
            (shape, f32),
            (shape, f32),
            ((steps, rows, lanes), fwd_acc.dtype),
        ],
        now,
        adjoint_later.reshape(shape),
        courant.reshape(shape),
        fwd_acc.reshape(steps, rows, lanes),
        surf_dest.reshape(1, entries),
        surf_cell.reshape(1, entries),
        surf_vals.reshape(steps, entries),
        flops=40 * rows * lanes,
        scratch=[
            pltpu.VMEM(shape, f32),
            pltpu.VMEM((1, entries), surf_dest.dtype),
            pltpu.VMEM((1, entries), surf_cell.dtype),
            pltpu.VMEM((steps, entries), f32),
            pltpu.SemaphoreType.DMA((7,)),
        ],
        in_hbm=range(7),
    )
    if everywhere:
        tables = [table] + [
            lax.ppermute(table, "tgt", [(i, i ^ far) for i in range(slabs)])
            for far in range(2, slabs, 2)
        ]
        inject = None
    else:
        tables = slotted_tables(table, surf_dest, slabs)
        inject = injection(here, tables, [[0]] * len(tables), steps, shape, False)
        part = part + inject[0]
        tables = []

    fixes, extra, later_field, grad = [], [], None, None
    for step in range(steps):
        last = step == steps - 1
        fix = everywhere and step == 1
        if step:
            outs = [(shape, f32)] * (2 + fix + last)
            args = [current, later_field, courant_here, fwd, inject[step]]
            args += [inject[0]] if fix else []
            args += [grad] if step > 1 else []
            part, grad, *extra = on_chip(
                functools.partial(own_kernel, planes, step, fix, last),
                outs,
                *args,
                flops=40 * rows * lanes,
            )
            if fix:
                current = extra.pop(0)
        carried = tables if step == 0 else []
        args = [here, *received, part, courant_here, *fixes]
        args += [*extra, grad] if last else []
        outs = [(shape, f32)] + ([(shape, f32)] if last else [])
        if carried:
            outs.append(((rows + len(carried) * table_rows, lanes), f32))
        fresh, *other = on_chip(
            functools.partial(halo_kernel, planes, slabs, fix, last, len(carried)),
            outs,
            *args,
            *carried,
            flops=10 * rows * lanes,
        )
        later_field, current, fixes = current, fresh, []
        if not last:
            received = exchange(other[0] if carried else fresh, fresh)
        if carried:
            places = [rows + i * table_rows for i in range(len(carried))]
            first_rows = [[0]] * len(carried) + [places]
            inject = injection(here, [*tables, received[0]], first_rows, steps, shape, True)
            fixes = inject[steps:]
    grad = sum_over(other[0], "shot")
    return (current.reshape(adjoint_now.shape), grad.reshape(courant.shape))


def solution(mesh):
    in_specs = (
        P(("grp", "shot"), "tgt", None, None),
        P(("grp", "shot"), "tgt", None, None),
        P("tgt", None, None),
        P(("grp", "shot"), None, "tgt", None, None),
        P("tgt", None),
        P("tgt"),
        P(("grp", "shot"), None, "tgt"),
    )
    out_specs = (P(("grp", "shot"), "tgt", None, None), P(("grp", "tgt"), None, None))
    return jax.shard_map(
        on_device, mesh=mesh, in_specs=in_specs, out_specs=out_specs, check_vma=False
    )
```

```python
import functools

import jax
import jax.numpy as jnp
from jax import lax
from jax.experimental import pallas as pl
from jax.experimental.pallas import tpu as pltpu
from jax.sharding import PartitionSpec as P

CAP = 128
GATHER_LIMIT = 4096
REACH = 4
PIECES = 3

COEFFS = (-205.0 / 72.0, 8.0 / 5.0, -1.0 / 5.0, 8.0 / 315.0, -1.0 / 560.0)


def on_chip(kernel, outs, *args, flops=0, scratch=(), in_hbm=()):
    spaces = [pltpu.SMEM if a.ndim == 1 else pltpu.VMEM for a in args]
    for i in in_hbm:
        spaces[i] = pltpu.HBM
    results = pl.pallas_call(
        kernel,
        out_shape=[pltpu.VMEM(shape, dtype) for shape, dtype in outs],
        in_specs=[pl.BlockSpec(memory_space=s) for s in spaces],
        out_specs=[pl.BlockSpec(memory_space=pltpu.VMEM) for _ in outs],
        scratch_shapes=list(scratch),
        cost_estimate=pl.CostEstimate(
            flops=flops,
            bytes_accessed=sum(a.size * a.dtype.itemsize for a in args),
            transcendentals=0,
        ),
    )(
        *[
            a if s is pltpu.SMEM else pltpu.with_memory_space_constraint(a, s)
            for a, s in zip(args, spaces)
        ]
    )
    return list(results)


def swap_pairs(count, first):
    partner = list(range(count))
    for left in range(first, count - 1, 2):
        partner[left], partner[left + 1] = left + 1, left
    return list(enumerate(partner))


def exchange(to_inner, to_outer):
    count = lax.axis_size("tgt")
    outer = lax.ppermute(to_outer, "tgt", swap_pairs(count, 1))
    inner = lax.ppermute(to_inner, "tgt", swap_pairs(count, 0))
    return inner, outer


def slotted_tables(table, surf_dest, owners):
    target = surf_dest[:, 0]
    onehot_table = (target[:, None] == jnp.arange(owners, dtype=jnp.int32)[None, :]).astype(
        jnp.int32
    )
    ranks = jnp.sum((jnp.cumsum(onehot_table, axis=0) - 1) * onehot_table, axis=1)
    position = target * CAP + ranks
    slots = jnp.full((table.shape[0], owners * CAP), -1.0, jnp.float32)
    slots = slots.at[:, position].set(table)
    arrived = lax.all_to_all(
        slots.reshape(-1, owners, CAP), "tgt", split_axis=1, concat_axis=1, tiled=True
    )
    flat = arrived.reshape(-1, owners * CAP)
    chunk = 1024 if owners * CAP % 1024 == 0 else CAP
    return [flat[:, i : i + chunk] for i in range(0, owners * CAP, chunk)]


def inject_kernel(steps, first_rows, with_halo, more, here_ref, *refs):
    table_refs, refs = refs[: len(first_rows)], refs[len(first_rows) :]
    in_refs, out_refs = (refs[: len(refs) // 2], refs[len(refs) // 2 :]) if more else ((), refs)
    rows, lanes = out_refs[0].shape
    here = here_ref[0].astype(jnp.float32)
    left, right = [], []
    for table_ref, firsts in zip(table_refs, first_rows):
        for first in firsts:
            table = table_ref[first : first + 2 + steps]
            count = table.shape[1]
            slab = table[0:1]
            cell = table[1:2].astype(jnp.int32)
            row, lane = cell // lanes, cell % lanes
            in_lane = lax.broadcasted_iota(jnp.int32, (lanes, count), 0) == lane
            spread = jnp.where(in_lane, 1.0, 0.0).astype(jnp.bfloat16)
            each_row = lax.broadcasted_iota(jnp.int32, (rows, count), 0)
            in_row = [each_row == jnp.where(slab == here, row, -1)]
            if with_halo:
                in_row.append(each_row == jnp.where(slab == here - 1.0, row, -1))
                in_row.append(each_row == jnp.where(slab == here + 1.0, row, -1))
            rest = [table[2 + step : 3 + step] for step in range(steps)]
            for _ in range(PIECES):
                part = [r.astype(jnp.bfloat16).astype(jnp.float32) for r in rest]
                rest = [r - p for r, p in zip(rest, part)]
                picks = [(in_row[0], p) for p in part] + [(m, part[0]) for m in in_row[1:]]
                left.append(
                    jnp.concatenate(
                        [jnp.where(m, p, 0.0).astype(jnp.bfloat16) for m, p in picks], axis=0
                    )
                )
                right.append(spread)
    total = lax.dot_general(
        jnp.concatenate(left, axis=1),
        jnp.concatenate(right, axis=1),
        (((1,), (1,)), ((), ())),
        preferred_element_type=jnp.float32,
    )
    for i, out_ref in enumerate(out_refs):
        mine = total[i * rows : (i + 1) * rows]
        out_ref[...] = in_refs[i][...] + mine if more else mine


def injection(here, tables, first_rows, steps, shape, with_halo, before=()):
    count = steps + 2 * with_halo
    entries = sum(t.shape[1] * len(f) for t, f in zip(tables, first_rows))
    return on_chip(
        functools.partial(inject_kernel, steps, first_rows, with_halo, len(before) > 0),
        [(shape, jnp.float32)] * count,
        here,
        *tables,
        *before,
        flops=4 * 2 * PIECES * count * shape[0] * shape[1] * entries,
    )


def plane_stencil(plane):
    cells_y, lanes = plane.shape
    at_y = lax.broadcasted_iota(jnp.int32, plane.shape, 0)
    at_z = lax.broadcasted_iota(jnp.int32, plane.shape, 1)
    total = 3.0 * COEFFS[0] * plane
    for k in range(1, REACH + 1):
        pairs = (
            jnp.where(at_y >= k, pltpu.roll(plane, k, 0), 0.0)
            + jnp.where(at_y < cells_y - k, pltpu.roll(plane, cells_y - k, 0), 0.0)
            + jnp.where(at_z >= k, pltpu.roll(plane, k, 1), 0.0)
            + jnp.where(at_z < lanes - k, pltpu.roll(plane, lanes - k, 1), 0.0)
        )
        total = total + COEFFS[k] * pairs
    return total


def own_part(current, p, later, courant):
    total = plane_stencil(current[p])
    for k in range(1, REACH + 1):
        for q in (p - k, p + k):
            if 0 <= q < len(current):
                total = total + COEFFS[k] * current[q]
    return 2.0 * current[p] - later + courant * courant * total


def first_kernel(planes, table_rows, *refs):
    refs = list(refs)
    now_hbm, later_hbm, courant_hbm, fwd_hbm, dest_hbm, cell_hbm, vals_hbm = refs[:7]
    part_ref, table_ref, now_ref, courant_ref, fwd_ref = refs[7:12]
    later_ref, dest_ref, cell_ref, vals_ref, sems = refs[12:]
    pairs = [
        (dest_hbm, dest_ref),
        (cell_hbm, cell_ref),
        (vals_hbm, vals_ref),
        (now_hbm, now_ref),
        (later_hbm, later_ref),
        (courant_hbm, courant_ref),
        (fwd_hbm, fwd_ref),
    ]
    copies = [pltpu.make_async_copy(a, b, sems.at[i]) for i, (a, b) in enumerate(pairs)]
    for copy in copies:
        copy.start()
    for copy in copies[:3]:
        copy.wait()
    table_ref[...] = jnp.zeros_like(table_ref)
    table_ref[0:1] = dest_ref[...].astype(jnp.float32)
    table_ref[1:2] = cell_ref[...].astype(jnp.float32)
    table_ref[2 : 2 + vals_ref.shape[0]] = vals_ref[...]
    for copy in copies[3:6]:
        copy.wait()
    cells_y = now_ref.shape[0] // planes
    at = [slice(p * cells_y, (p + 1) * cells_y) for p in range(planes)]
    current = [now_ref[s] for s in at]
    for p, s in enumerate(at):
        part_ref[s] = own_part(current, p, later_ref[s], courant_ref[s])
    copies[6].wait()


def own_kernel(planes, step, fix_inject, last, *refs):
    refs = list(refs)
    current_ref, later_ref, courant_ref, fwd_ref, inject_ref = refs[:5]
    refs = refs[5:]
    fix_ref = refs.pop(0) if fix_inject else None
    grad_in_ref = refs.pop(0) if step > 1 else None
    part_ref = refs.pop(0)
    grad_ref = refs.pop(0)
    fixed_ref = refs.pop(0) if fix_inject else None
    weight_ref = refs.pop(0) if last else None
    cells_y = current_ref.shape[0] // planes
    at = [slice(p * cells_y, (p + 1) * cells_y) for p in range(planes)]
    current = [current_ref[s] for s in at]
    if fix_inject:
        current = [c + fix_ref[s] for c, s in zip(current, at)]
        for c, s in zip(current, at):
            fixed_ref[s] = c
    for p, s in enumerate(at):
        courant = courant_ref[s]
        part_ref[s] = own_part(current, p, later_ref[s], courant) + inject_ref[s]
        grad = fwd_ref[step - 1, s].astype(jnp.float32) * current[p]
        if step > 1:
            grad = grad + grad_in_ref[s]
        if last:
            inverse = 1.0 / courant
            grad = grad * inverse
            weight_ref[s] = fwd_ref[step, s].astype(jnp.float32) * inverse
        grad_ref[s] = grad


def halo_kernel(planes, slabs, fix_inject, last, tables, here_ref, *refs):
    refs = list(refs)
    inner_ref, outer_ref, part_ref, courant_ref = refs[:4]
    refs = refs[4:]
    fix_refs = (refs.pop(0), refs.pop(0)) if fix_inject else None
    weight_ref, grad_in_ref = (refs.pop(0), refs.pop(0)) if last else (None, None)
    table_refs = [refs.pop(0) for _ in range(tables)]
    fresh_ref = refs.pop(0)
    other_ref = refs.pop(0) if last or tables else None
    here = here_ref[0]
    even = here % 2 == 0
    rows = part_ref.shape[0]
    cells_y = rows // planes
    at = [slice(p * cells_y, (p + 1) * cells_y) for p in range(planes)]
    low, high = {}, {}
    for p in range(planes - REACH, planes):
        plane = jnp.where(even, outer_ref[at[p]], inner_ref[at[p]])
        if fix_inject:
            plane = plane + fix_refs[0][at[p]]
        low[p - planes] = jnp.where(here == 0, 0.0, plane)
    for p in range(REACH):
        plane = jnp.where(even, inner_ref[at[p]], outer_ref[at[p]])
        if fix_inject:
            plane = plane + fix_refs[1][at[p]]
        high[p + planes] = jnp.where(here == slabs - 1, 0.0, plane)
    for p, s in enumerate(at):
        terms = []
        for k in range(1, REACH + 1):
            if p - k < 0:
                terms.append(COEFFS[k] * low[p - k])
            if p + k >= planes:
                terms.append(COEFFS[k] * high[p + k])
        courant = courant_ref[s]
        fresh = part_ref[s] + courant * courant * sum(terms[1:], terms[0])
        fresh_ref[s] = fresh
        if last:
            other_ref[s] = grad_in_ref[s] + weight_ref[s] * fresh
        if tables:
            other_ref[s] = fresh
    for i, table_ref in enumerate(table_refs):
        first = rows + i * table_ref.shape[0]
        other_ref[first : first + table_ref.shape[0]] = table_ref[...]


def sum_over(value, axis):
    count = lax.axis_size(axis)
    if count & (count - 1):
        return lax.psum(value, axis)
    distance = count // 2
    while distance:
        value = value + lax.ppermute(value, axis, [(i, i ^ distance) for i in range(count)])
        distance //= 2
    return value


def on_device(adjoint_now, adjoint_later, courant, fwd_acc, surf_dest, surf_cell, surf_vals):
    planes, cells_y, lanes = courant.shape
    steps = fwd_acc.shape[1]
    rows = planes * cells_y
    shape = (rows, lanes)
    entries = surf_cell.shape[0]
    slabs = lax.axis_size("tgt")
    here = lax.axis_index("tgt").reshape(1)
    now = adjoint_now.reshape(shape)
    table_rows = -(-(2 + steps) // 8) * 8
    everywhere = (
        slabs & (slabs - 1) == 0 and slabs * entries <= GATHER_LIMIT and entries == lanes
    )

    received = exchange(now, now)
    f32 = jnp.float32
    part, table, current, courant_here, fwd = on_chip(
        functools.partial(first_kernel, planes, table_rows),
        [
            (shape, f32),
            ((table_rows, entries), f32),
            (shape, f32),
            (shape, f32),
            ((steps, rows, lanes), fwd_acc.dtype),
        ],
        now,
        adjoint_later.reshape(shape),
        courant.reshape(shape),
        fwd_acc.reshape(steps, rows, lanes),
        surf_dest.reshape(1, entries),
        surf_cell.reshape(1, entries),
        surf_vals.reshape(steps, entries),
        flops=40 * rows * lanes,
        scratch=[
            pltpu.VMEM(shape, f32),
            pltpu.VMEM((1, entries), surf_dest.dtype),
            pltpu.VMEM((1, entries), surf_cell.dtype),
            pltpu.VMEM((steps, entries), f32),
            pltpu.SemaphoreType.DMA((7,)),
        ],
        in_hbm=range(7),
    )
    if everywhere:
        tables = [table] + [
            lax.ppermute(table, "tgt", [(i, i ^ far) for i in range(slabs)])
            for far in range(2, slabs)
        ]
        inject = None
    else:
        tables = slotted_tables(table, surf_dest, slabs)
        inject = injection(here, tables, [[0]] * len(tables), steps, shape, False)
        part = part + inject[0]
        tables = []

    fixes, extra, later_field, grad = [], [], None, None
    for step in range(steps):
        last = step == steps - 1
        fix = everywhere and step == 1
        if step:
            outs = [(shape, f32)] * (2 + fix + last)
            args = [current, later_field, courant_here, fwd, inject[step]]
            args += [inject[0]] if fix else []
            args += [grad] if step > 1 else []
            part, grad, *extra = on_chip(
                functools.partial(own_kernel, planes, step, fix, last),
                outs,
                *args,
                flops=40 * rows * lanes,
            )
            if fix:
                current = extra.pop(0)
        carried = tables[:1] if step == 0 else []
        args = [here, *received, part, courant_here, *fixes]
        args += [*extra, grad] if last else []
        outs = [(shape, f32)] + ([(shape, f32)] if last else [])
        if carried:
            outs.append(((rows + len(carried) * table_rows, lanes), f32))
        fresh, *other = on_chip(
            functools.partial(halo_kernel, planes, slabs, fix, last, len(carried)),
            outs,
            *args,
            *carried,
            flops=10 * rows * lanes,
        )
        later_field, current, fixes = current, fresh, []
        if not last:
            received = exchange(other[0] if carried else fresh, fresh)
        if carried:
            inject = injection(here, tables, [[0]] * len(tables), steps, shape, True)
            inject = injection(here, received[:1], [[rows]], steps, shape, True, inject)
            fixes = inject[steps:]
    grad = sum_over(other[0], "shot")
    return (current.reshape(adjoint_now.shape), grad.reshape(courant.shape))


def solution(mesh):
    in_specs = (
        P(("grp", "shot"), "tgt", None, None),
        P(("grp", "shot"), "tgt", None, None),
        P("tgt", None, None),
        P(("grp", "shot"), None, "tgt", None, None),
        P("tgt", None),
        P("tgt"),
        P(("grp", "shot"), None, "tgt"),
    )
    out_specs = (P(("grp", "shot"), "tgt", None, None), P(("grp", "tgt"), None, None))
    return jax.shard_map(
        on_device, mesh=mesh, in_specs=in_specs, out_specs=out_specs, check_vma=False
    )
```

```python
import functools

import jax
import jax.numpy as jnp
from jax import lax
from jax.experimental import pallas as pl
from jax.experimental.pallas import tpu as pltpu
from jax.sharding import PartitionSpec as P

CAP = 128
GATHER_LIMIT = 4096
REACH = 4
PIECES = 3

COEFFS = (-205.0 / 72.0, 8.0 / 5.0, -1.0 / 5.0, 8.0 / 315.0, -1.0 / 560.0)


def on_chip(kernel, outs, *args, flops=0, scratch=(), in_hbm=()):
    spaces = [pltpu.SMEM if a.ndim == 1 else pltpu.VMEM for a in args]
    for i in in_hbm:
        spaces[i] = pltpu.HBM
    results = pl.pallas_call(
        kernel,
        out_shape=[pltpu.VMEM(shape, dtype) for shape, dtype in outs],
        in_specs=[pl.BlockSpec(memory_space=s) for s in spaces],
        out_specs=[pl.BlockSpec(memory_space=pltpu.VMEM) for _ in outs],
        scratch_shapes=list(scratch),
        cost_estimate=pl.CostEstimate(
            flops=flops,
            bytes_accessed=sum(a.size * a.dtype.itemsize for a in args),
            transcendentals=0,
        ),
    )(
        *[
            a if s is pltpu.SMEM else pltpu.with_memory_space_constraint(a, s)
            for a, s in zip(args, spaces)
        ]
    )
    return list(results)


def swap_pairs(count, shots, first):
    routes = []
    for slab in range(count):
        paired = slab >= first and (slab - first) // 2 * 2 + first + 1 < count
        partner = slab + 1 - 2 * ((slab - first) % 2) if paired else slab
        for shot in range(shots):
            other = shot if paired or shots % 2 else shot ^ 1
            routes.append((slab * shots + shot, partner * shots + other))
    return routes


def exchange(to_inner, to_outer):
    count, shots = lax.axis_size("tgt"), lax.axis_size("shot")
    outer = lax.ppermute(to_outer, ("tgt", "shot"), swap_pairs(count, shots, 1))
    inner = lax.ppermute(to_inner, ("tgt", "shot"), swap_pairs(count, shots, 0))
    return inner, outer


def slotted_tables(table, surf_dest, owners):
    target = surf_dest[:, 0]
    onehot_table = (target[:, None] == jnp.arange(owners, dtype=jnp.int32)[None, :]).astype(
        jnp.int32
    )
    ranks = jnp.sum((jnp.cumsum(onehot_table, axis=0) - 1) * onehot_table, axis=1)
    position = target * CAP + ranks
    slots = jnp.full((table.shape[0], owners * CAP), -1.0, jnp.float32)
    slots = slots.at[:, position].set(table)
    arrived = lax.all_to_all(
        slots.reshape(-1, owners, CAP), "tgt", split_axis=1, concat_axis=1, tiled=True
    )
    flat = arrived.reshape(-1, owners * CAP)
    chunk = 1024 if owners * CAP % 1024 == 0 else CAP
    return [flat[:, i : i + chunk] for i in range(0, owners * CAP, chunk)]


def inject_kernel(steps, first_rows, with_halo, more, here_ref, *refs):
    table_refs, refs = refs[: len(first_rows)], refs[len(first_rows) :]
    in_refs, out_refs = (refs[: len(refs) // 2], refs[len(refs) // 2 :]) if more else ((), refs)
    rows, lanes = out_refs[0].shape
    here = here_ref[0].astype(jnp.float32)
    left, right = [], []
    for table_ref, firsts in zip(table_refs, first_rows):
        for first in firsts:
            table = table_ref[first : first + 2 + steps]
            count = table.shape[1]
            slab = table[0:1]
            cell = table[1:2].astype(jnp.int32)
            row, lane = cell // lanes, cell % lanes
            in_lane = lax.broadcasted_iota(jnp.int32, (lanes, count), 0) == lane
            spread = jnp.where(in_lane, 1.0, 0.0).astype(jnp.bfloat16)
            each_row = lax.broadcasted_iota(jnp.int32, (rows, count), 0)
            in_row = [each_row == jnp.where(slab == here, row, -1)]
            if with_halo:
                in_row.append(each_row == jnp.where(slab == here - 1.0, row, -1))
                in_row.append(each_row == jnp.where(slab == here + 1.0, row, -1))
            rest = [table[2 + step : 3 + step] for step in range(steps)]
            for _ in range(PIECES):
                part = [r.astype(jnp.bfloat16).astype(jnp.float32) for r in rest]
                rest = [r - p for r, p in zip(rest, part)]
                picks = [(in_row[0], p) for p in part] + [(m, part[0]) for m in in_row[1:]]
                left.append(
                    jnp.concatenate(
                        [jnp.where(m, p, 0.0).astype(jnp.bfloat16) for m, p in picks], axis=0
                    )
                )
                right.append(spread)
    total = lax.dot_general(
        jnp.concatenate(left, axis=1),
        jnp.concatenate(right, axis=1),
        (((1,), (1,)), ((), ())),
        preferred_element_type=jnp.float32,
    )
    for i, out_ref in enumerate(out_refs):
        mine = total[i * rows : (i + 1) * rows]
        out_ref[...] = in_refs[i][...] + mine if more else mine


def injection(here, tables, first_rows, steps, shape, with_halo, before=()):
    count = steps + 2 * with_halo
    entries = sum(t.shape[1] * len(f) for t, f in zip(tables, first_rows))
    return on_chip(
        functools.partial(inject_kernel, steps, first_rows, with_halo, len(before) > 0),
        [(shape, jnp.float32)] * count,
        here,
        *tables,
        *before,
        flops=4 * 2 * PIECES * count * shape[0] * shape[1] * entries,
    )


def plane_stencil(plane):
    cells_y, lanes = plane.shape
    at_y = lax.broadcasted_iota(jnp.int32, plane.shape, 0)
    at_z = lax.broadcasted_iota(jnp.int32, plane.shape, 1)
    total = 3.0 * COEFFS[0] * plane
    for k in range(1, REACH + 1):
        pairs = (
            jnp.where(at_y >= k, pltpu.roll(plane, k, 0), 0.0)
            + jnp.where(at_y < cells_y - k, pltpu.roll(plane, cells_y - k, 0), 0.0)
            + jnp.where(at_z >= k, pltpu.roll(plane, k, 1), 0.0)
            + jnp.where(at_z < lanes - k, pltpu.roll(plane, lanes - k, 1), 0.0)
        )
        total = total + COEFFS[k] * pairs
    return total


def own_part(current, p, later, courant):
    total = plane_stencil(current[p])
    for k in range(1, REACH + 1):
        for q in (p - k, p + k):
            if 0 <= q < len(current):
                total = total + COEFFS[k] * current[q]
    return 2.0 * current[p] - later + courant * courant * total


def first_kernel(planes, table_rows, *refs):
    refs = list(refs)
    now_hbm, later_hbm, courant_hbm, fwd_hbm, dest_hbm, cell_hbm, vals_hbm = refs[:7]
    part_ref, table_ref, now_ref, courant_ref, fwd_ref = refs[7:12]
    later_ref, dest_ref, cell_ref, vals_ref, sems = refs[12:]
    pairs = [
        (dest_hbm, dest_ref),
        (cell_hbm, cell_ref),
        (vals_hbm, vals_ref),
        (now_hbm, now_ref),
        (later_hbm, later_ref),
        (courant_hbm, courant_ref),
        (fwd_hbm, fwd_ref),
    ]
    copies = [pltpu.make_async_copy(a, b, sems.at[i]) for i, (a, b) in enumerate(pairs)]
    for copy in copies:
        copy.start()
    for copy in copies[:3]:
        copy.wait()
    table_ref[...] = jnp.zeros_like(table_ref)
    table_ref[0:1] = dest_ref[...].astype(jnp.float32)
    table_ref[1:2] = cell_ref[...].astype(jnp.float32)
    table_ref[2 : 2 + vals_ref.shape[0]] = vals_ref[...]
    for copy in copies[3:6]:
        copy.wait()
    cells_y = now_ref.shape[0] // planes
    at = [slice(p * cells_y, (p + 1) * cells_y) for p in range(planes)]
    current = [now_ref[s] for s in at]
    for p, s in enumerate(at):
        part_ref[s] = own_part(current, p, later_ref[s], courant_ref[s])
    copies[6].wait()


def own_kernel(planes, step, fix_inject, last, *refs):
    refs = list(refs)
    current_ref, later_ref, courant_ref, fwd_ref, inject_ref = refs[:5]
    refs = refs[5:]
    fix_ref = refs.pop(0) if fix_inject else None
    grad_in_ref = refs.pop(0) if step > 1 else None
    part_ref = refs.pop(0)
    grad_ref = refs.pop(0)
    fixed_ref = refs.pop(0) if fix_inject else None
    weight_ref = refs.pop(0) if last else None
    cells_y = current_ref.shape[0] // planes
    at = [slice(p * cells_y, (p + 1) * cells_y) for p in range(planes)]
    current = [current_ref[s] for s in at]
    if fix_inject:
        current = [c + fix_ref[s] for c, s in zip(current, at)]
        for c, s in zip(current, at):
            fixed_ref[s] = c
    for p, s in enumerate(at):
        courant = courant_ref[s]
        part_ref[s] = own_part(current, p, later_ref[s], courant) + inject_ref[s]
        grad = fwd_ref[step - 1, s].astype(jnp.float32) * current[p]
        if step > 1:
            grad = grad + grad_in_ref[s]
        if last:
            inverse = 1.0 / courant
            grad = grad * inverse
            weight_ref[s] = fwd_ref[step, s].astype(jnp.float32) * inverse
        grad_ref[s] = grad


def halo_kernel(planes, slabs, fix_inject, last, tables, here_ref, *refs):
    refs = list(refs)
    inner_ref, outer_ref, part_ref, courant_ref = refs[:4]
    refs = refs[4:]
    fix_refs = (refs.pop(0), refs.pop(0)) if fix_inject else None
    weight_ref, grad_in_ref = (refs.pop(0), refs.pop(0)) if last else (None, None)
    table_refs = [refs.pop(0) for _ in range(tables)]
    fresh_ref = refs.pop(0)
    other_ref = refs.pop(0) if last or tables else None
    here = here_ref[0]
    even = here % 2 == 0
    rows = part_ref.shape[0]
    cells_y = rows // planes
    at = [slice(p * cells_y, (p + 1) * cells_y) for p in range(planes)]
    low, high = {}, {}
    for p in range(planes - REACH, planes):
        plane = jnp.where(even, outer_ref[at[p]], inner_ref[at[p]])
        if fix_inject:
            plane = plane + fix_refs[0][at[p]]
        low[p - planes] = jnp.where(here == 0, 0.0, plane)
    for p in range(REACH):
        plane = jnp.where(even, inner_ref[at[p]], outer_ref[at[p]])
        if fix_inject:
            plane = plane + fix_refs[1][at[p]]
        high[p + planes] = jnp.where(here == slabs - 1, 0.0, plane)
    for p, s in enumerate(at):
        terms = []
        for k in range(1, REACH + 1):
            if p - k < 0:
                terms.append(COEFFS[k] * low[p - k])
            if p + k >= planes:
                terms.append(COEFFS[k] * high[p + k])
        courant = courant_ref[s]
        fresh = part_ref[s] + courant * courant * sum(terms[1:], terms[0])
        fresh_ref[s] = fresh
        if last:
            other_ref[s] = grad_in_ref[s] + weight_ref[s] * fresh
        if tables:
            other_ref[s] = fresh
    for i, table_ref in enumerate(table_refs):
        first = rows + i * table_ref.shape[0]
        other_ref[first : first + table_ref.shape[0]] = table_ref[...]


def sum_over(value, axis):
    count = lax.axis_size(axis)
    if count & (count - 1):
        return lax.psum(value, axis)
    distance = count // 2
    while distance:
        value = value + lax.ppermute(value, axis, [(i, i ^ distance) for i in range(count)])
        distance //= 2
    return value


def on_device(adjoint_now, adjoint_later, courant, fwd_acc, surf_dest, surf_cell, surf_vals):
    planes, cells_y, lanes = courant.shape
    steps = fwd_acc.shape[1]
    rows = planes * cells_y
    shape = (rows, lanes)
    entries = surf_cell.shape[0]
    slabs = lax.axis_size("tgt")
    here = lax.axis_index("tgt").reshape(1)
    now = adjoint_now.reshape(shape)
    table_rows = -(-(2 + steps) // 8) * 8
    everywhere = (
        slabs & (slabs - 1) == 0 and slabs * entries <= GATHER_LIMIT and entries == lanes
    )

    received = exchange(now, now)
    f32 = jnp.float32
    part, table, current, courant_here, fwd = on_chip(
        functools.partial(first_kernel, planes, table_rows),
        [
            (shape, f32),
            ((table_rows, entries), f32),
            (shape, f32),
            (shape, f32),
            ((steps, rows, lanes), fwd_acc.dtype),
        ],
        now,
        adjoint_later.reshape(shape),
        courant.reshape(shape),
        fwd_acc.reshape(steps, rows, lanes),
        surf_dest.reshape(1, entries),
        surf_cell.reshape(1, entries),
        surf_vals.reshape(steps, entries),
        flops=40 * rows * lanes,
        scratch=[
            pltpu.VMEM(shape, f32),
            pltpu.VMEM((1, entries), surf_dest.dtype),
            pltpu.VMEM((1, entries), surf_cell.dtype),
            pltpu.VMEM((steps, entries), f32),
            pltpu.SemaphoreType.DMA((7,)),
        ],
        in_hbm=range(7),
    )
    if everywhere:
        tables = [table] + [
            lax.ppermute(table, "tgt", [(i, i ^ far) for i in range(slabs)])
            for far in range(2, slabs)
        ]
        inject = None
    else:
        tables = slotted_tables(table, surf_dest, slabs)
        inject = injection(here, tables, [[0]] * len(tables), steps, shape, False)
        part = part + inject[0]
        tables = []

    fixes, extra, later_field, grad = [], [], None, None
    for step in range(steps):
        last = step == steps - 1
        fix = everywhere and step == 1
        if step:
            outs = [(shape, f32)] * (2 + fix + last)
            args = [current, later_field, courant_here, fwd, inject[step]]
            args += [inject[0]] if fix else []
            args += [grad] if step > 1 else []
            part, grad, *extra = on_chip(
                functools.partial(own_kernel, planes, step, fix, last),
                outs,
                *args,
                flops=40 * rows * lanes,
            )
            if fix:
                current = extra.pop(0)
        carried = tables[:1] if step == 0 else []
        args = [here, *received, part, courant_here, *fixes]
        args += [*extra, grad] if last else []
        outs = [(shape, f32)] + ([(shape, f32)] if last else [])
        if carried:
            outs.append(((rows + len(carried) * table_rows, lanes), f32))
        fresh, *other = on_chip(
            functools.partial(halo_kernel, planes, slabs, fix, last, len(carried)),
            outs,
            *args,
            *carried,
            flops=10 * rows * lanes,
        )
        later_field, current, fixes = current, fresh, []
        if not last:
            received = exchange(other[0] if carried else fresh, fresh)
        if carried:
            inject = injection(here, tables, [[0]] * len(tables), steps, shape, True)
            inject = injection(here, received[:1], [[rows]], steps, shape, True, inject)
            fixes = inject[steps:]
    grad = sum_over(other[0], "shot")
    return (current.reshape(adjoint_now.shape), grad.reshape(courant.shape))


def solution(mesh):
    in_specs = (
        P(("grp", "shot"), "tgt", None, None),
        P(("grp", "shot"), "tgt", None, None),
        P("tgt", None, None),
        P(("grp", "shot"), None, "tgt", None, None),
        P("tgt", None),
        P("tgt"),
        P(("grp", "shot"), None, "tgt"),
    )
    out_specs = (P(("grp", "shot"), "tgt", None, None), P(("grp", "tgt"), None, None))
    return jax.shard_map(
        on_device, mesh=mesh, in_specs=in_specs, out_specs=out_specs, check_vma=False
    )
```

```python
import functools

import jax
import jax.numpy as jnp
from jax import lax
from jax.experimental import pallas as pl
from jax.experimental.pallas import tpu as pltpu
from jax.sharding import PartitionSpec as P

CAP = 128
GATHER_LIMIT = 4096
REACH = 4
PIECES = 3

COEFFS = (-205.0 / 72.0, 8.0 / 5.0, -1.0 / 5.0, 8.0 / 315.0, -1.0 / 560.0)


def on_chip(kernel, outs, *args, flops=0, scratch=(), in_hbm=()):
    spaces = [pltpu.SMEM if a.ndim == 1 else pltpu.VMEM for a in args]
    for i in in_hbm:
        spaces[i] = pltpu.HBM
    results = pl.pallas_call(
        kernel,
        out_shape=[pltpu.VMEM(shape, dtype) for shape, dtype in outs],
        in_specs=[pl.BlockSpec(memory_space=s) for s in spaces],
        out_specs=[pl.BlockSpec(memory_space=pltpu.VMEM) for _ in outs],
        scratch_shapes=list(scratch),
        cost_estimate=pl.CostEstimate(
            flops=flops,
            bytes_accessed=sum(a.size * a.dtype.itemsize for a in args),
            transcendentals=0,
        ),
    )(
        *[
            a if s is pltpu.SMEM else pltpu.with_memory_space_constraint(a, s)
            for a, s in zip(args, spaces)
        ]
    )
    return list(results)


def swap_pairs(count, shots, first):
    routes = []
    for slab in range(count):
        paired = slab >= first and (slab - first) // 2 * 2 + first + 1 < count
        partner = slab + 1 - 2 * ((slab - first) % 2) if paired else slab
        for shot in range(shots):
            other = shot if paired or shots % 2 else shot ^ 1
            routes.append((slab * shots + shot, partner * shots + other))
    return routes


def exchange(to_inner, to_outer):
    count, shots = lax.axis_size("tgt"), lax.axis_size("shot")
    outer = lax.ppermute(to_outer, ("tgt", "shot"), swap_pairs(count, shots, 1))
    inner = lax.ppermute(to_inner, ("tgt", "shot"), swap_pairs(count, shots, 0))
    return inner, outer


def slotted_tables(table, surf_dest, owners):
    target = surf_dest[:, 0]
    onehot_table = (target[:, None] == jnp.arange(owners, dtype=jnp.int32)[None, :]).astype(
        jnp.int32
    )
    ranks = jnp.sum((jnp.cumsum(onehot_table, axis=0) - 1) * onehot_table, axis=1)
    position = target * CAP + ranks
    slots = jnp.full((table.shape[0], owners * CAP), -1.0, jnp.float32)
    slots = slots.at[:, position].set(table)
    arrived = lax.all_to_all(
        slots.reshape(-1, owners, CAP), "tgt", split_axis=1, concat_axis=1, tiled=True
    )
    flat = arrived.reshape(-1, owners * CAP)
    chunk = 1024 if owners * CAP % 1024 == 0 else CAP
    return [flat[:, i : i + chunk] for i in range(0, owners * CAP, chunk)]


def inject_kernel(steps, first_rows, with_halo, more, here_ref, *refs):
    table_refs, refs = refs[: len(first_rows)], refs[len(first_rows) :]
    in_refs, out_refs = (refs[: len(refs) // 2], refs[len(refs) // 2 :]) if more else ((), refs)
    rows, lanes = out_refs[0].shape
    here = here_ref[0].astype(jnp.float32)
    left, right = [], []
    for table_ref, firsts in zip(table_refs, first_rows):
        for first in firsts:
            table = table_ref[first : first + 2 + steps]
            count = table.shape[1]
            slab = table[0:1]
            cell = table[1:2].astype(jnp.int32)
            row, lane = cell // lanes, cell % lanes
            in_lane = lax.broadcasted_iota(jnp.int32, (lanes, count), 0) == lane
            spread = jnp.where(in_lane, 1.0, 0.0).astype(jnp.bfloat16)
            each_row = lax.broadcasted_iota(jnp.int32, (rows, count), 0)
            in_row = [each_row == jnp.where(slab == here, row, -1)]
            if with_halo:
                in_row.append(each_row == jnp.where(slab == here - 1.0, row, -1))
                in_row.append(each_row == jnp.where(slab == here + 1.0, row, -1))
            rest = [table[2 + step : 3 + step] for step in range(steps)]
            for _ in range(PIECES):
                part = [r.astype(jnp.bfloat16).astype(jnp.float32) for r in rest]
                rest = [r - p for r, p in zip(rest, part)]
                picks = [(in_row[0], p) for p in part] + [(m, part[0]) for m in in_row[1:]]
                left.append(
                    jnp.concatenate(
                        [jnp.where(m, p, 0.0).astype(jnp.bfloat16) for m, p in picks], axis=0
                    )
                )
                right.append(spread)
    total = lax.dot_general(
        jnp.concatenate(left, axis=1),
        jnp.concatenate(right, axis=1),
        (((1,), (1,)), ((), ())),
        preferred_element_type=jnp.float32,
    )
    for i, out_ref in enumerate(out_refs):
        mine = total[i * rows : (i + 1) * rows]
        out_ref[...] = in_refs[i][...] + mine if more else mine


def injection(here, tables, first_rows, steps, shape, with_halo, before=()):
    count = steps + 2 * with_halo
    entries = sum(t.shape[1] * len(f) for t, f in zip(tables, first_rows))
    return on_chip(
        functools.partial(inject_kernel, steps, first_rows, with_halo, len(before) > 0),
        [(shape, jnp.float32)] * count,
        here,
        *tables,
        *before,
        flops=4 * 2 * PIECES * count * shape[0] * shape[1] * entries,
    )


def plane_stencil(plane):
    cells_y, lanes = plane.shape
    at_y = lax.broadcasted_iota(jnp.int32, plane.shape, 0)
    at_z = lax.broadcasted_iota(jnp.int32, plane.shape, 1)
    total = 3.0 * COEFFS[0] * plane
    for k in range(1, REACH + 1):
        pairs = (
            jnp.where(at_y >= k, pltpu.roll(plane, k, 0), 0.0)
            + jnp.where(at_y < cells_y - k, pltpu.roll(plane, cells_y - k, 0), 0.0)
            + jnp.where(at_z >= k, pltpu.roll(plane, k, 1), 0.0)
            + jnp.where(at_z < lanes - k, pltpu.roll(plane, lanes - k, 1), 0.0)
        )
        total = total + COEFFS[k] * pairs
    return total


def own_part(current, p, later, courant):
    total = plane_stencil(current[p])
    for k in range(1, REACH + 1):
        for q in (p - k, p + k):
            if 0 <= q < len(current):
                total = total + COEFFS[k] * current[q]
    return 2.0 * current[p] - later + courant * courant * total


def pack_kernel(dest_hbm, cell_hbm, vals_hbm, table_ref, dest_ref, cell_ref, vals_ref, sems):
    pairs = [(dest_hbm, dest_ref), (cell_hbm, cell_ref), (vals_hbm, vals_ref)]
    copies = [pltpu.make_async_copy(a, b, sems.at[i]) for i, (a, b) in enumerate(pairs)]
    for copy in copies:
        copy.start()
    table_ref[...] = jnp.zeros_like(table_ref)
    for copy in copies:
        copy.wait()
    table_ref[0:1] = dest_ref[...].astype(jnp.float32)
    table_ref[1:2] = cell_ref[...].astype(jnp.float32)
    table_ref[2 : 2 + vals_ref.shape[0]] = vals_ref[...]


def first_kernel(planes, *refs):
    now_hbm, later_hbm, courant_hbm, fwd_hbm = refs[:4]
    part_ref, now_ref, courant_ref, fwd_ref, later_ref, sems = refs[4:]
    pairs = [
        (now_hbm, now_ref),
        (later_hbm, later_ref),
        (courant_hbm, courant_ref),
        (fwd_hbm, fwd_ref),
    ]
    copies = [pltpu.make_async_copy(a, b, sems.at[i]) for i, (a, b) in enumerate(pairs)]
    for copy in copies:
        copy.start()
    for copy in copies[:3]:
        copy.wait()
    cells_y = now_ref.shape[0] // planes
    at = [slice(p * cells_y, (p + 1) * cells_y) for p in range(planes)]
    current = [now_ref[s] for s in at]
    for p, s in enumerate(at):
        part_ref[s] = own_part(current, p, later_ref[s], courant_ref[s])
    copies[3].wait()


def own_kernel(planes, step, fix_inject, last, *refs):
    refs = list(refs)
    current_ref, later_ref, courant_ref, fwd_ref, inject_ref = refs[:5]
    refs = refs[5:]
    fix_ref = refs.pop(0) if fix_inject else None
    grad_in_ref = refs.pop(0) if step > 1 else None
    part_ref = refs.pop(0)
    grad_ref = refs.pop(0)
    fixed_ref = refs.pop(0) if fix_inject else None
    weight_ref = refs.pop(0) if last else None
    cells_y = current_ref.shape[0] // planes
    at = [slice(p * cells_y, (p + 1) * cells_y) for p in range(planes)]
    current = [current_ref[s] for s in at]
    if fix_inject:
        current = [c + fix_ref[s] for c, s in zip(current, at)]
        for c, s in zip(current, at):
            fixed_ref[s] = c
    for p, s in enumerate(at):
        courant = courant_ref[s]
        part_ref[s] = own_part(current, p, later_ref[s], courant) + inject_ref[s]
        grad = fwd_ref[step - 1, s].astype(jnp.float32) * current[p]
        if step > 1:
            grad = grad + grad_in_ref[s]
        if last:
            inverse = 1.0 / courant
            grad = grad * inverse
            weight_ref[s] = fwd_ref[step, s].astype(jnp.float32) * inverse
        grad_ref[s] = grad


def halo_kernel(planes, slabs, fix_inject, last, tables, here_ref, *refs):
    refs = list(refs)
    inner_ref, outer_ref, part_ref, courant_ref = refs[:4]
    refs = refs[4:]
    fix_refs = (refs.pop(0), refs.pop(0)) if fix_inject else None
    weight_ref, grad_in_ref = (refs.pop(0), refs.pop(0)) if last else (None, None)
    table_refs = [refs.pop(0) for _ in range(tables)]
    fresh_ref = refs.pop(0)
    other_ref = refs.pop(0) if last or tables else None
    here = here_ref[0]
    even = here % 2 == 0
    rows = part_ref.shape[0]
    cells_y = rows // planes
    at = [slice(p * cells_y, (p + 1) * cells_y) for p in range(planes)]
    low, high = {}, {}
    for p in range(planes - REACH, planes):
        plane = jnp.where(even, outer_ref[at[p]], inner_ref[at[p]])
        if fix_inject:
            plane = plane + fix_refs[0][at[p]]
        low[p - planes] = jnp.where(here == 0, 0.0, plane)
    for p in range(REACH):
        plane = jnp.where(even, inner_ref[at[p]], outer_ref[at[p]])
        if fix_inject:
            plane = plane + fix_refs[1][at[p]]
        high[p + planes] = jnp.where(here == slabs - 1, 0.0, plane)
    for p, s in enumerate(at):
        terms = []
        for k in range(1, REACH + 1):
            if p - k < 0:
                terms.append(COEFFS[k] * low[p - k])
            if p + k >= planes:
                terms.append(COEFFS[k] * high[p + k])
        courant = courant_ref[s]
        fresh = part_ref[s] + courant * courant * sum(terms[1:], terms[0])
        fresh_ref[s] = fresh
        if last:
            other_ref[s] = grad_in_ref[s] + weight_ref[s] * fresh
        if tables:
            other_ref[s] = fresh
    for i, table_ref in enumerate(table_refs):
        first = rows + i * table_ref.shape[0]
        other_ref[first : first + table_ref.shape[0]] = table_ref[...]


def sum_over(value, axis):
    count = lax.axis_size(axis)
    if count & (count - 1):
        return lax.psum(value, axis)
    distance = count // 2
    while distance:
        value = value + lax.ppermute(value, axis, [(i, i ^ (2 * distance - 1)) for i in range(count)])
        distance //= 2
    return value


def on_device(adjoint_now, adjoint_later, courant, fwd_acc, surf_dest, surf_cell, surf_vals):
    planes, cells_y, lanes = courant.shape
    steps = fwd_acc.shape[1]
    rows = planes * cells_y
    shape = (rows, lanes)
    entries = surf_cell.shape[0]
    slabs = lax.axis_size("tgt")
    here = lax.axis_index("tgt").reshape(1)
    now = adjoint_now.reshape(shape)
    table_rows = -(-(2 + steps) // 8) * 8
    everywhere = (
        slabs & (slabs - 1) == 0 and slabs * entries <= GATHER_LIMIT and entries == lanes
    )

    received = exchange(now, now)
    f32 = jnp.float32
    (table,) = on_chip(
        pack_kernel,
        [((table_rows, entries), f32)],
        surf_dest.reshape(1, entries),
        surf_cell.reshape(1, entries),
        surf_vals.reshape(steps, entries),
        scratch=[
            pltpu.VMEM((1, entries), surf_dest.dtype),
            pltpu.VMEM((1, entries), surf_cell.dtype),
            pltpu.VMEM((steps, entries), f32),
            pltpu.SemaphoreType.DMA((3,)),
        ],
        in_hbm=range(3),
    )
    part, current, courant_here, fwd = on_chip(
        functools.partial(first_kernel, planes),
        [(shape, f32), (shape, f32), (shape, f32), ((steps, rows, lanes), fwd_acc.dtype)],
        now,
        adjoint_later.reshape(shape),
        courant.reshape(shape),
        fwd_acc.reshape(steps, rows, lanes),
        flops=40 * rows * lanes,
        scratch=[pltpu.VMEM(shape, f32), pltpu.SemaphoreType.DMA((4,))],
        in_hbm=range(4),
    )
    if everywhere:
        tables = [table] + [
            lax.ppermute(table, "tgt", [(i, i ^ far) for i in range(slabs)])
            for far in range(2, slabs)
        ]
        inject = None
    else:
        tables = slotted_tables(table, surf_dest, slabs)
        inject = injection(here, tables, [[0]] * len(tables), steps, shape, False)
        part = part + inject[0]
        tables = []

    fixes, extra, later_field, grad = [], [], None, None
    for step in range(steps):
        last = step == steps - 1
        fix = everywhere and step == 1
        if step:
            outs = [(shape, f32)] * (2 + fix + last)
            args = [current, later_field, courant_here, fwd, inject[step]]
            args += [inject[0]] if fix else []
            args += [grad] if step > 1 else []
            part, grad, *extra = on_chip(
                functools.partial(own_kernel, planes, step, fix, last),
                outs,
                *args,
                flops=40 * rows * lanes,
            )
            if fix:
                current = extra.pop(0)
        carried = tables[:1] if step == 0 else []
        args = [here, *received, part, courant_here, *fixes]
        args += [*extra, grad] if last else []
        outs = [(shape, f32)] + ([(shape, f32)] if last else [])
        if carried:
            outs.append(((rows + len(carried) * table_rows, lanes), f32))
        fresh, *other = on_chip(
            functools.partial(halo_kernel, planes, slabs, fix, last, len(carried)),
            outs,
            *args,
            *carried,
            flops=10 * rows * lanes,
        )
        later_field, current, fixes = current, fresh, []
        if not last:
            received = exchange(other[0] if carried else fresh, fresh)
        if carried:
            inject = injection(here, tables, [[0]] * len(tables), steps, shape, True)
            inject = injection(here, received[:1], [[rows]], steps, shape, True, inject)
            fixes = inject[steps:]
    grad = sum_over(other[0], "shot")
    return (current.reshape(adjoint_now.shape), grad.reshape(courant.shape))


def solution(mesh):
    in_specs = (
        P(("grp", "shot"), "tgt", None, None),
        P(("grp", "shot"), "tgt", None, None),
        P("tgt", None, None),
        P(("grp", "shot"), None, "tgt", None, None),
        P("tgt", None),
        P("tgt"),
        P(("grp", "shot"), None, "tgt"),
    )
    out_specs = (P(("grp", "shot"), "tgt", None, None), P(("grp", "tgt"), None, None))
    return jax.shard_map(
        on_device, mesh=mesh, in_specs=in_specs, out_specs=out_specs, check_vma=False
    )
```

```python
import functools

import jax
import jax.numpy as jnp
from jax import lax
from jax.experimental import pallas as pl
from jax.experimental.pallas import tpu as pltpu
from jax.sharding import PartitionSpec as P

CAP = 128
GATHER_LIMIT = 4096
REACH = 4
PIECES = 3

COEFFS = (-205.0 / 72.0, 8.0 / 5.0, -1.0 / 5.0, 8.0 / 315.0, -1.0 / 560.0)


def on_chip(kernel, outs, *args, flops=0, scratch=(), in_hbm=()):
    spaces = [pltpu.SMEM if a.ndim == 1 else pltpu.VMEM for a in args]
    for i in in_hbm:
        spaces[i] = pltpu.HBM
    results = pl.pallas_call(
        kernel,
        out_shape=[pltpu.VMEM(shape, dtype) for shape, dtype in outs],
        in_specs=[pl.BlockSpec(memory_space=s) for s in spaces],
        out_specs=[pl.BlockSpec(memory_space=pltpu.VMEM) for _ in outs],
        scratch_shapes=list(scratch),
        cost_estimate=pl.CostEstimate(
            flops=flops,
            bytes_accessed=sum(a.size * a.dtype.itemsize for a in args),
            transcendentals=0,
        ),
    )(
        *[
            a if s is pltpu.SMEM else pltpu.with_memory_space_constraint(a, s)
            for a, s in zip(args, spaces)
        ]
    )
    return list(results)


def swap_pairs(count, shots, first):
    routes = []
    for slab in range(count):
        paired = slab >= first and (slab - first) // 2 * 2 + first + 1 < count
        partner = slab + 1 - 2 * ((slab - first) % 2) if paired else slab
        for shot in range(shots):
            other = shot if paired or shots % 2 else shot ^ 1
            routes.append((slab * shots + shot, partner * shots + other))
    return routes


def exchange(to_inner, to_outer):
    count, shots = lax.axis_size("tgt"), lax.axis_size("shot")
    outer = lax.ppermute(to_outer, ("tgt", "shot"), swap_pairs(count, shots, 1))
    inner = lax.ppermute(to_inner, ("tgt", "shot"), swap_pairs(count, shots, 0))
    return inner, outer


def slotted_tables(table, surf_dest, owners):
    target = surf_dest[:, 0]
    onehot_table = (target[:, None] == jnp.arange(owners, dtype=jnp.int32)[None, :]).astype(
        jnp.int32
    )
    ranks = jnp.sum((jnp.cumsum(onehot_table, axis=0) - 1) * onehot_table, axis=1)
    position = target * CAP + ranks
    slots = jnp.full((table.shape[0], owners * CAP), -1.0, jnp.float32)
    slots = slots.at[:, position].set(table)
    arrived = lax.all_to_all(
        slots.reshape(-1, owners, CAP), "tgt", split_axis=1, concat_axis=1, tiled=True
    )
    flat = arrived.reshape(-1, owners * CAP)
    chunk = 1024 if owners * CAP % 1024 == 0 else CAP
    return [flat[:, i : i + chunk] for i in range(0, owners * CAP, chunk)]


def inject_kernel(steps, first_rows, with_halo, more, here_ref, *refs):
    table_refs, refs = refs[: len(first_rows)], refs[len(first_rows) :]
    in_refs, out_refs = (refs[: len(refs) // 2], refs[len(refs) // 2 :]) if more else ((), refs)
    rows, lanes = out_refs[0].shape
    here = here_ref[0].astype(jnp.float32)
    left, right = [], []
    for table_ref, firsts in zip(table_refs, first_rows):
        for first in firsts:
            table = table_ref[first : first + 2 + steps]
            count = table.shape[1]
            slab = table[0:1]
            cell = table[1:2].astype(jnp.int32)
            row, lane = cell // lanes, cell % lanes
            in_lane = lax.broadcasted_iota(jnp.int32, (lanes, count), 0) == lane
            spread = jnp.where(in_lane, 1.0, 0.0).astype(jnp.bfloat16)
            each_row = lax.broadcasted_iota(jnp.int32, (rows, count), 0)
            in_row = [each_row == jnp.where(slab == here, row, -1)]
            if with_halo:
                in_row.append(each_row == jnp.where(slab == here - 1.0, row, -1))
                in_row.append(each_row == jnp.where(slab == here + 1.0, row, -1))
            rest = [table[2 + step : 3 + step] for step in range(steps)]
            for _ in range(PIECES):
                part = [r.astype(jnp.bfloat16).astype(jnp.float32) for r in rest]
                rest = [r - p for r, p in zip(rest, part)]
                picks = [(in_row[0], p) for p in part] + [(m, part[0]) for m in in_row[1:]]
                left.append(
                    jnp.concatenate(
                        [jnp.where(m, p, 0.0).astype(jnp.bfloat16) for m, p in picks], axis=0
                    )
                )
                right.append(spread)
    total = lax.dot_general(
        jnp.concatenate(left, axis=1),
        jnp.concatenate(right, axis=1),
        (((1,), (1,)), ((), ())),
        preferred_element_type=jnp.float32,
    )
    for i, out_ref in enumerate(out_refs):
        mine = total[i * rows : (i + 1) * rows]
        out_ref[...] = in_refs[i][...] + mine if more else mine


def injection(here, tables, first_rows, steps, shape, with_halo, before=()):
    count = steps + 2 * with_halo
    entries = sum(t.shape[1] * len(f) for t, f in zip(tables, first_rows))
    return on_chip(
        functools.partial(inject_kernel, steps, first_rows, with_halo, len(before) > 0),
        [(shape, jnp.float32)] * count,
        here,
        *tables,
        *before,
        flops=4 * 2 * PIECES * count * shape[0] * shape[1] * entries,
    )


def plane_stencil(plane):
    cells_y, lanes = plane.shape
    at_y = lax.broadcasted_iota(jnp.int32, plane.shape, 0)
    at_z = lax.broadcasted_iota(jnp.int32, plane.shape, 1)
    total = 3.0 * COEFFS[0] * plane
    for k in range(1, REACH + 1):
        pairs = (
            jnp.where(at_y >= k, pltpu.roll(plane, k, 0), 0.0)
            + jnp.where(at_y < cells_y - k, pltpu.roll(plane, cells_y - k, 0), 0.0)
            + jnp.where(at_z >= k, pltpu.roll(plane, k, 1), 0.0)
            + jnp.where(at_z < lanes - k, pltpu.roll(plane, lanes - k, 1), 0.0)
        )
        total = total + COEFFS[k] * pairs
    return total


def own_part(current, p, later, courant):
    total = plane_stencil(current[p])
    for k in range(1, REACH + 1):
        for q in (p - k, p + k):
            if 0 <= q < len(current):
                total = total + COEFFS[k] * current[q]
    return 2.0 * current[p] - later + courant * courant * total


def first_kernel(planes, table_rows, *refs):
    refs = list(refs)
    now_hbm, later_hbm, courant_hbm, fwd_hbm, dest_hbm, cell_hbm, vals_hbm = refs[:7]
    part_ref, table_ref, now_ref, courant_ref, fwd_ref = refs[7:12]
    later_ref, dest_ref, cell_ref, vals_ref, sems = refs[12:]
    pairs = [
        (dest_hbm, dest_ref),
        (cell_hbm, cell_ref),
        (vals_hbm, vals_ref),
        (now_hbm, now_ref),
        (later_hbm, later_ref),
        (courant_hbm, courant_ref),
        (fwd_hbm, fwd_ref),
    ]
    copies = [pltpu.make_async_copy(a, b, sems.at[i]) for i, (a, b) in enumerate(pairs)]
    for copy in copies:
        copy.start()
    for copy in copies[:3]:
        copy.wait()
    table_ref[...] = jnp.zeros_like(table_ref)
    table_ref[0:1] = dest_ref[...].astype(jnp.float32)
    table_ref[1:2] = cell_ref[...].astype(jnp.float32)
    table_ref[2 : 2 + vals_ref.shape[0]] = vals_ref[...]
    for copy in copies[3:6]:
        copy.wait()
    cells_y = now_ref.shape[0] // planes
    at = [slice(p * cells_y, (p + 1) * cells_y) for p in range(planes)]
    current = [now_ref[s] for s in at]
    for p, s in enumerate(at):
        part_ref[s] = own_part(current, p, later_ref[s], courant_ref[s])
    copies[6].wait()


def own_kernel(planes, step, fix_inject, last, *refs):
    refs = list(refs)
    current_ref, later_ref, courant_ref, fwd_ref, inject_ref = refs[:5]
    refs = refs[5:]
    fix_ref = refs.pop(0) if fix_inject else None
    grad_in_ref = refs.pop(0) if step > 1 else None
    part_ref = refs.pop(0)
    grad_ref = refs.pop(0)
    fixed_ref = refs.pop(0) if fix_inject else None
    weight_ref = refs.pop(0) if last else None
    cells_y = current_ref.shape[0] // planes
    at = [slice(p * cells_y, (p + 1) * cells_y) for p in range(planes)]
    current = [current_ref[s] for s in at]
    if fix_inject:
        current = [c + fix_ref[s] for c, s in zip(current, at)]
        for c, s in zip(current, at):
            fixed_ref[s] = c
    for p, s in enumerate(at):
        courant = courant_ref[s]
        part_ref[s] = own_part(current, p, later_ref[s], courant) + inject_ref[s]
        grad = fwd_ref[step - 1, s].astype(jnp.float32) * current[p]
        if step > 1:
            grad = grad + grad_in_ref[s]
        if last:
            inverse = 1.0 / courant
            grad = grad * inverse
            weight_ref[s] = fwd_ref[step, s].astype(jnp.float32) * inverse
        grad_ref[s] = grad


def halo_kernel(planes, slabs, fix_inject, last, tables, here_ref, *refs):
    refs = list(refs)
    inner_ref, outer_ref, part_ref, courant_ref = refs[:4]
    refs = refs[4:]
    fix_refs = (refs.pop(0), refs.pop(0)) if fix_inject else None
    weight_ref, grad_in_ref = (refs.pop(0), refs.pop(0)) if last else (None, None)
    table_refs = [refs.pop(0) for _ in range(tables)]
    fresh_ref = refs.pop(0)
    other_ref = refs.pop(0) if last or tables else None
    here = here_ref[0]
    even = here % 2 == 0
    rows = part_ref.shape[0]
    cells_y = rows // planes
    at = [slice(p * cells_y, (p + 1) * cells_y) for p in range(planes)]
    low, high = {}, {}
    for p in range(planes - REACH, planes):
        plane = jnp.where(even, outer_ref[at[p]], inner_ref[at[p]])
        if fix_inject:
            plane = plane + fix_refs[0][at[p]]
        low[p - planes] = jnp.where(here == 0, 0.0, plane)
    for p in range(REACH):
        plane = jnp.where(even, inner_ref[at[p]], outer_ref[at[p]])
        if fix_inject:
            plane = plane + fix_refs[1][at[p]]
        high[p + planes] = jnp.where(here == slabs - 1, 0.0, plane)
    for p, s in enumerate(at):
        terms = []
        for k in range(1, REACH + 1):
            if p - k < 0:
                terms.append(COEFFS[k] * low[p - k])
            if p + k >= planes:
                terms.append(COEFFS[k] * high[p + k])
        courant = courant_ref[s]
        fresh = part_ref[s] + courant * courant * sum(terms[1:], terms[0])
        fresh_ref[s] = fresh
        if last:
            other_ref[s] = grad_in_ref[s] + weight_ref[s] * fresh
        if tables:
            other_ref[s] = fresh
    for i, table_ref in enumerate(table_refs):
        first = rows + i * table_ref.shape[0]
        other_ref[first : first + table_ref.shape[0]] = table_ref[...]


def sum_over(value, axis):
    count = lax.axis_size(axis)
    if count & (count - 1):
        return lax.psum(value, axis)
    distance = count // 2
    while distance:
        value = value + lax.ppermute(value, axis, [(i, i ^ distance) for i in range(count)])
        distance //= 2
    return value


def on_device(adjoint_now, adjoint_later, courant, fwd_acc, surf_dest, surf_cell, surf_vals):
    planes, cells_y, lanes = courant.shape
    steps = fwd_acc.shape[1]
    rows = planes * cells_y
    shape = (rows, lanes)
    entries = surf_cell.shape[0]
    slabs = lax.axis_size("tgt")
    here = lax.axis_index("tgt").reshape(1)
    now = adjoint_now.reshape(shape)
    table_rows = -(-(2 + steps) // 8) * 8
    everywhere = (
        slabs & (slabs - 1) == 0 and slabs * entries <= GATHER_LIMIT and entries == lanes
    )

    received = exchange(now, now)
    f32 = jnp.float32
    part, table, current, courant_here, fwd = on_chip(
        functools.partial(first_kernel, planes, table_rows),
        [
            (shape, f32),
            ((table_rows, entries), f32),
            (shape, f32),
            (shape, f32),
            ((steps, rows, lanes), fwd_acc.dtype),
        ],
        now,
        adjoint_later.reshape(shape),
        courant.reshape(shape),
        fwd_acc.reshape(steps, rows, lanes),
        surf_dest.reshape(1, entries),
        surf_cell.reshape(1, entries),
        surf_vals.reshape(steps, entries),
        flops=40 * rows * lanes,
        scratch=[
            pltpu.VMEM(shape, f32),
            pltpu.VMEM((1, entries), surf_dest.dtype),
            pltpu.VMEM((1, entries), surf_cell.dtype),
            pltpu.VMEM((steps, entries), f32),
            pltpu.SemaphoreType.DMA((7,)),
        ],
        in_hbm=range(7),
    )
    if everywhere:
        tables = [table] + [
            lax.ppermute(table, "tgt", [(i, i ^ far) for i in range(slabs)])
            for far in reversed(range(2, slabs))
        ]
        inject = None
    else:
        tables = slotted_tables(table, surf_dest, slabs)
        inject = injection(here, tables, [[0]] * len(tables), steps, shape, False)
        part = part + inject[0]
        tables = []

    fixes, extra, later_field, grad = [], [], None, None
    for step in range(steps):
        last = step == steps - 1
        fix = everywhere and step == 1
        if step:
            outs = [(shape, f32)] * (2 + fix + last)
            args = [current, later_field, courant_here, fwd, inject[step]]
            args += [inject[0]] if fix else []
            args += [grad] if step > 1 else []
            part, grad, *extra = on_chip(
                functools.partial(own_kernel, planes, step, fix, last),
                outs,
                *args,
                flops=40 * rows * lanes,
            )
            if fix:
                current = extra.pop(0)
        carried = tables[:1] if step == 0 else []
        args = [here, *received, part, courant_here, *fixes]
        args += [*extra, grad] if last else []
        outs = [(shape, f32)] + ([(shape, f32)] if last else [])
        if carried:
            outs.append(((rows + len(carried) * table_rows, lanes), f32))
        fresh, *other = on_chip(
            functools.partial(halo_kernel, planes, slabs, fix, last, len(carried)),
            outs,
            *args,
            *carried,
            flops=10 * rows * lanes,
        )
        later_field, current, fixes = current, fresh, []
        if not last:
            received = exchange(other[0] if carried else fresh, fresh)
        if carried:
            inject = injection(here, tables, [[0]] * len(tables), steps, shape, True)
            inject = injection(here, received[:1], [[rows]], steps, shape, True, inject)
            fixes = inject[steps:]
    grad = sum_over(other[0], "shot")
    return (current.reshape(adjoint_now.shape), grad.reshape(courant.shape))


def solution(mesh):
    in_specs = (
        P(("grp", "shot"), "tgt", None, None),
        P(("grp", "shot"), "tgt", None, None),
        P("tgt", None, None),
        P(("grp", "shot"), None, "tgt", None, None),
        P("tgt", None),
        P("tgt"),
        P(("grp", "shot"), None, "tgt"),
    )
    out_specs = (P(("grp", "shot"), "tgt", None, None), P(("grp", "tgt"), None, None))
    return jax.shard_map(
        on_device, mesh=mesh, in_specs=in_specs, out_specs=out_specs, check_vma=False
    )
```

```python
import functools

import jax
import jax.numpy as jnp
from jax import lax
from jax.experimental import pallas as pl
from jax.experimental.pallas import tpu as pltpu
from jax.sharding import PartitionSpec as P

CAP = 128
GATHER_LIMIT = 4096
REACH = 4
PIECES = 3
EFFORT = 4

COEFFS = (-205.0 / 72.0, 8.0 / 5.0, -1.0 / 5.0, 8.0 / 315.0, -1.0 / 560.0)


def on_chip(kernel, outs, *args, flops=0, scratch=(), in_hbm=()):
    spaces = [pltpu.SMEM if a.ndim == 1 else pltpu.VMEM for a in args]
    for i in in_hbm:
        spaces[i] = pltpu.HBM
    results = pl.pallas_call(
        kernel,
        out_shape=[pltpu.VMEM(shape, dtype) for shape, dtype in outs],
        in_specs=[pl.BlockSpec(memory_space=s) for s in spaces],
        out_specs=[pl.BlockSpec(memory_space=pltpu.VMEM) for _ in outs],
        scratch_shapes=list(scratch),
        cost_estimate=pl.CostEstimate(
            flops=flops,
            bytes_accessed=sum(a.size * a.dtype.itemsize for a in args),
            transcendentals=0,
        ),
    )(
        *[
            a if s is pltpu.SMEM else pltpu.with_memory_space_constraint(a, s)
            for a, s in zip(args, spaces)
        ]
    )
    return list(results)


def swap_pairs(count, shots, first):
    routes = []
    for slab in range(count):
        paired = slab >= first and (slab - first) // 2 * 2 + first + 1 < count
        partner = slab + 1 - 2 * ((slab - first) % 2) if paired else slab
        for shot in range(shots):
            other = shot if paired or shots % 2 else shot ^ 1
            routes.append((slab * shots + shot, partner * shots + other))
    return routes


def exchange(slab):
    count, shots = lax.axis_size("tgt"), lax.axis_size("shot")
    outer = lax.ppermute(slab, ("tgt", "shot"), swap_pairs(count, shots, 1))
    inner = lax.ppermute(slab, ("tgt", "shot"), swap_pairs(count, shots, 0))
    return inner, outer


def slotted_tables(table, surf_dest, owners):
    target = surf_dest[:, 0]
    onehot_table = (target[:, None] == jnp.arange(owners, dtype=jnp.int32)[None, :]).astype(
        jnp.int32
    )
    ranks = jnp.sum((jnp.cumsum(onehot_table, axis=0) - 1) * onehot_table, axis=1)
    position = target * CAP + ranks
    slots = jnp.full((table.shape[0], owners * CAP), -1.0, jnp.float32)
    slots = slots.at[:, position].set(table)
    arrived = lax.all_to_all(
        slots.reshape(-1, owners, CAP), "tgt", split_axis=1, concat_axis=1, tiled=True
    )
    flat = arrived.reshape(-1, owners * CAP)
    chunk = 1024 if owners * CAP % 1024 == 0 else CAP
    return [flat[:, i : i + chunk] for i in range(0, owners * CAP, chunk)]


def inject_kernel(steps, table_count, with_halo, here_ref, *refs):
    table_refs, out_refs = refs[:table_count], refs[table_count:]
    rows, lanes = out_refs[0].shape
    here = here_ref[0].astype(jnp.float32)
    left, right = [], []
    for table_ref in table_refs:
        table = table_ref[...]
        count = table.shape[1]
        slab = table[0:1]
        cell = table[1:2].astype(jnp.int32)
        row, lane = cell // lanes, cell % lanes
        in_lane = lax.broadcasted_iota(jnp.int32, (lanes, count), 0) == lane
        spread = jnp.where(in_lane, 1.0, 0.0).astype(jnp.bfloat16)
        each_row = lax.broadcasted_iota(jnp.int32, (rows, count), 0)
        in_row = [each_row == jnp.where(slab == here, row, -1)]
        if with_halo:
            in_row.append(each_row == jnp.where(slab == here - 1.0, row, -1))
            in_row.append(each_row == jnp.where(slab == here + 1.0, row, -1))
        rest = [table[2 + step : 3 + step] for step in range(steps)]
        for _ in range(PIECES):
            part = [r.astype(jnp.bfloat16).astype(jnp.float32) for r in rest]
            rest = [r - p for r, p in zip(rest, part)]
            picks = [(in_row[0], p) for p in part] + [(m, part[0]) for m in in_row[1:]]
            left.append(
                jnp.concatenate(
                    [jnp.where(m, p, 0.0).astype(jnp.bfloat16) for m, p in picks], axis=0
                )
            )
            right.append(spread)
    total = lax.dot_general(
        jnp.concatenate(left, axis=1),
        jnp.concatenate(right, axis=1),
        (((1,), (1,)), ((), ())),
        preferred_element_type=jnp.float32,
    )
    for i, out_ref in enumerate(out_refs):
        out_ref[...] = total[i * rows : (i + 1) * rows]


def injection(here, tables, steps, shape, with_halo):
    count = steps + 2 * with_halo
    entries = sum(t.shape[1] for t in tables)
    return on_chip(
        functools.partial(inject_kernel, steps, len(tables), with_halo),
        [(shape, jnp.float32)] * count,
        here,
        *tables,
        flops=EFFORT * 2 * PIECES * count * shape[0] * shape[1] * entries,
    )


def plane_stencil(plane):
    cells_y, lanes = plane.shape
    at_y = lax.broadcasted_iota(jnp.int32, plane.shape, 0)
    at_z = lax.broadcasted_iota(jnp.int32, plane.shape, 1)
    total = 3.0 * COEFFS[0] * plane
    for k in range(1, REACH + 1):
        pairs = (
            jnp.where(at_y >= k, pltpu.roll(plane, k, 0), 0.0)
            + jnp.where(at_y < cells_y - k, pltpu.roll(plane, cells_y - k, 0), 0.0)
            + jnp.where(at_z >= k, pltpu.roll(plane, k, 1), 0.0)
            + jnp.where(at_z < lanes - k, pltpu.roll(plane, lanes - k, 1), 0.0)
        )
        total = total + COEFFS[k] * pairs
    return total


def own_part(current, p, later, courant):
    total = plane_stencil(current[p])
    for k in range(1, REACH + 1):
        for q in (p - k, p + k):
            if 0 <= q < len(current):
                total = total + COEFFS[k] * current[q]
    return 2.0 * current[p] - later + courant * courant * total


def first_kernel(planes, table_rows, *refs):
    refs = list(refs)
    now_hbm, later_hbm, courant_hbm, fwd_hbm, dest_hbm, cell_hbm, vals_hbm = refs[:7]
    part_ref, table_ref, now_ref, courant_ref, fwd_ref = refs[7:12]
    later_ref, dest_ref, cell_ref, vals_ref, sems = refs[12:]
    pairs = [
        (dest_hbm, dest_ref),
        (cell_hbm, cell_ref),
        (vals_hbm, vals_ref),
        (now_hbm, now_ref),
        (later_hbm, later_ref),
        (courant_hbm, courant_ref),
        (fwd_hbm, fwd_ref),
    ]
    copies = [pltpu.make_async_copy(a, b, sems.at[i]) for i, (a, b) in enumerate(pairs)]
    for copy in copies:
        copy.start()
    for copy in copies[:3]:
        copy.wait()
    table_ref[...] = jnp.zeros_like(table_ref)
    table_ref[0:1] = dest_ref[...].astype(jnp.float32)
    table_ref[1:2] = cell_ref[...].astype(jnp.float32)
    table_ref[2 : 2 + vals_ref.shape[0]] = vals_ref[...]
    for copy in copies[3:6]:
        copy.wait()
    cells_y = now_ref.shape[0] // planes
    at = [slice(p * cells_y, (p + 1) * cells_y) for p in range(planes)]
    current = [now_ref[s] for s in at]
    for p, s in enumerate(at):
        part_ref[s] = own_part(current, p, later_ref[s], courant_ref[s])
    copies[6].wait()


def own_kernel(planes, step, fix_inject, last, *refs):
    refs = list(refs)
    current_ref, later_ref, courant_ref, fwd_ref, inject_ref = refs[:5]
    refs = refs[5:]
    fix_ref = refs.pop(0) if fix_inject else None
    grad_in_ref = refs.pop(0) if step > 1 else None
    part_ref = refs.pop(0)
    grad_ref = refs.pop(0)
    fixed_ref = refs.pop(0) if fix_inject else None
    weight_ref = refs.pop(0) if last else None
    cells_y = current_ref.shape[0] // planes
    at = [slice(p * cells_y, (p + 1) * cells_y) for p in range(planes)]
    current = [current_ref[s] for s in at]
    if fix_inject:
        current = [c + fix_ref[s] for c, s in zip(current, at)]
        for c, s in zip(current, at):
            fixed_ref[s] = c
    for p, s in enumerate(at):
        courant = courant_ref[s]
        part_ref[s] = own_part(current, p, later_ref[s], courant) + inject_ref[s]
        grad = fwd_ref[step - 1, s].astype(jnp.float32) * current[p]
        if step > 1:
            grad = grad + grad_in_ref[s]
        if last:
            inverse = 1.0 / courant
            grad = grad * inverse
            weight_ref[s] = fwd_ref[step, s].astype(jnp.float32) * inverse
        grad_ref[s] = grad


def halo_kernel(planes, slabs, fix_inject, last, here_ref, *refs):
    refs = list(refs)
    inner_ref, outer_ref, part_ref, courant_ref = refs[:4]
    if last:
        inner_ref, outer_ref = outer_ref, inner_ref
    refs = refs[4:]
    fix_refs = (refs.pop(0), refs.pop(0)) if fix_inject else None
    weight_ref, grad_in_ref = (refs.pop(0), refs.pop(0)) if last else (None, None)
    fresh_ref = refs.pop(0)
    grad_ref = refs.pop(0) if last else None
    here = here_ref[0]
    even = here % 2 == 0
    rows = part_ref.shape[0]
    cells_y = rows // planes
    at = [slice(p * cells_y, (p + 1) * cells_y) for p in range(planes)]
    low, high = {}, {}
    for p in range(planes - REACH, planes):
        plane = jnp.where(even, outer_ref[at[p]], inner_ref[at[p]])
        if fix_inject:
            plane = plane + fix_refs[0][at[p]]
        low[p - planes] = jnp.where(here == 0, 0.0, plane)
    for p in range(REACH):
        plane = jnp.where(even, inner_ref[at[p]], outer_ref[at[p]])
        if fix_inject:
            plane = plane + fix_refs[1][at[p]]
        high[p + planes] = jnp.where(here == slabs - 1, 0.0, plane)
    for p, s in enumerate(at):
        terms = []
        for k in range(1, REACH + 1):
            if p - k < 0:
                terms.append(COEFFS[k] * low[p - k])
            if p + k >= planes:
                terms.append(COEFFS[k] * high[p + k])
        courant = courant_ref[s]
        fresh = part_ref[s] + courant * courant * sum(terms[1:], terms[0])
        fresh_ref[s] = fresh
        if last:
            grad_ref[s] = grad_in_ref[s] + weight_ref[s] * fresh


def sum_over(value, axis):
    count = lax.axis_size(axis)
    if count & (count - 1):
        return lax.psum(value, axis)
    distance = count // 2
    while distance:
        value = value + lax.ppermute(value, axis, [(i, i ^ distance) for i in range(count)])
        distance //= 2
    return value


def on_device(adjoint_now, adjoint_later, courant, fwd_acc, surf_dest, surf_cell, surf_vals):
    planes, cells_y, lanes = courant.shape
    steps = fwd_acc.shape[1]
    rows = planes * cells_y
    shape = (rows, lanes)
    entries = surf_cell.shape[0]
    slabs = lax.axis_size("tgt")
    here = lax.axis_index("tgt").reshape(1)
    now = adjoint_now.reshape(shape)
    table_rows = -(-(2 + steps) // 8) * 8
    everywhere = slabs & (slabs - 1) == 0 and slabs * entries <= GATHER_LIMIT

    received = exchange(now)
    f32 = jnp.float32
    part, table, current, courant_here, fwd = on_chip(
        functools.partial(first_kernel, planes, table_rows),
        [
            (shape, f32),
            ((table_rows, entries), f32),
            (shape, f32),
            (shape, f32),
            ((steps, rows, lanes), fwd_acc.dtype),
        ],
        now,
        adjoint_later.reshape(shape),
        courant.reshape(shape),
        fwd_acc.reshape(steps, rows, lanes),
        surf_dest.reshape(1, entries),
        surf_cell.reshape(1, entries),
        surf_vals.reshape(steps, entries),
        flops=40 * rows * lanes,
        scratch=[
            pltpu.VMEM(shape, f32),
            pltpu.VMEM((1, entries), surf_dest.dtype),
            pltpu.VMEM((1, entries), surf_cell.dtype),
            pltpu.VMEM((steps, entries), f32),
            pltpu.SemaphoreType.DMA((7,)),
        ],
        in_hbm=range(7),
    )
    if everywhere:
        tables = [table] + [
            lax.ppermute(table, "tgt", [(i, i ^ far) for i in range(slabs)])
            for far in [*range(slabs - 1, 2, -1), *range(1, min(slabs, 3))]
        ]
        inject = None
    else:
        tables = slotted_tables(table, surf_dest, slabs)
        inject = injection(here, tables, steps, shape, False)
        part = part + inject[0]
        tables = []

    fixes, extra, later_field, grad = [], [], None, None
    for step in range(steps):
        last = step == steps - 1
        fix = everywhere and step == 1
        if step:
            outs = [(shape, f32)] * (2 + fix + last)
            args = [current, later_field, courant_here, fwd, inject[step]]
            args += [inject[0]] if fix else []
            args += [grad] if step > 1 else []
            part, grad, *extra = on_chip(
                functools.partial(own_kernel, planes, step, fix, last),
                outs,
                *args,
                flops=40 * rows * lanes,
            )
            if fix:
                current = extra.pop(0)
        args = [here, *(received[::-1] if last else received), part, courant_here, *fixes]
        args += [*extra, grad] if last else []
        fresh, *other = on_chip(
            functools.partial(halo_kernel, planes, slabs, fix, last),
            [(shape, f32)] * (1 + last),
            *args,
            flops=10 * rows * lanes,
        )
        later_field, current, fixes = current, fresh, []
        if not last:
            received = exchange(fresh)
        if everywhere and step == 0:
            inject = injection(here, tables, steps, shape, True)
            fixes = inject[steps:]
    grad = sum_over(other[0], "shot")
    return (current.reshape(adjoint_now.shape), grad.reshape(courant.shape))


def solution(mesh):
    in_specs = (
        P(("grp", "shot"), "tgt", None, None),
        P(("grp", "shot"), "tgt", None, None),
        P("tgt", None, None),
        P(("grp", "shot"), None, "tgt", None, None),
        P("tgt", None),
        P("tgt"),
        P(("grp", "shot"), None, "tgt"),
    )
    out_specs = (P(("grp", "shot"), "tgt", None, None), P(("grp", "tgt"), None, None))
    return jax.shard_map(
        on_device, mesh=mesh, in_specs=in_specs, out_specs=out_specs, check_vma=False
    )
```

```python
import functools

import jax
import jax.numpy as jnp
from jax import lax
from jax.experimental import pallas as pl
from jax.experimental.pallas import tpu as pltpu
from jax.sharding import PartitionSpec as P

CAP = 128
GATHER_LIMIT = 4096
REACH = 4
PIECES = 3
EFFORT = 4

COEFFS = (-205.0 / 72.0, 8.0 / 5.0, -1.0 / 5.0, 8.0 / 315.0, -1.0 / 560.0)


def on_chip(kernel, outs, *args, flops=0, scratch=(), in_hbm=()):
    spaces = [pltpu.SMEM if a.ndim == 1 else pltpu.VMEM for a in args]
    for i in in_hbm:
        spaces[i] = pltpu.HBM
    results = pl.pallas_call(
        kernel,
        out_shape=[pltpu.VMEM(shape, dtype) for shape, dtype in outs],
        in_specs=[pl.BlockSpec(memory_space=s) for s in spaces],
        out_specs=[pl.BlockSpec(memory_space=pltpu.VMEM) for _ in outs],
        scratch_shapes=list(scratch),
        cost_estimate=pl.CostEstimate(
            flops=flops,
            bytes_accessed=sum(a.size * a.dtype.itemsize for a in args),
            transcendentals=0,
        ),
    )(
        *[
            a if s is pltpu.SMEM else pltpu.with_memory_space_constraint(a, s)
            for a, s in zip(args, spaces)
        ]
    )
    return list(results)


def swap_pairs(count, shots, first):
    routes = []
    for slab in range(count):
        paired = slab >= first and (slab - first) // 2 * 2 + first + 1 < count
        partner = slab + 1 - 2 * ((slab - first) % 2) if paired else slab
        for shot in range(shots):
            other = shot if paired or shots % 2 else shot ^ 1
            routes.append((slab * shots + shot, partner * shots + other))
    return routes


def exchange(slab, other=None):
    count, shots = lax.axis_size("tgt"), lax.axis_size("shot")
    outer = lax.ppermute(slab if other is None else other, ("tgt", "shot"), swap_pairs(count, shots, 1))
    inner = lax.ppermute(slab, ("tgt", "shot"), swap_pairs(count, shots, 0))
    return inner, outer


def slotted_tables(table, surf_dest, owners):
    target = surf_dest[:, 0]
    onehot_table = (target[:, None] == jnp.arange(owners, dtype=jnp.int32)[None, :]).astype(
        jnp.int32
    )
    ranks = jnp.sum((jnp.cumsum(onehot_table, axis=0) - 1) * onehot_table, axis=1)
    position = target * CAP + ranks
    slots = jnp.full((table.shape[0], owners * CAP), -1.0, jnp.float32)
    slots = slots.at[:, position].set(table)
    arrived = lax.all_to_all(
        slots.reshape(-1, owners, CAP), "tgt", split_axis=1, concat_axis=1, tiled=True
    )
    flat = arrived.reshape(-1, owners * CAP)
    chunk = 1024 if owners * CAP % 1024 == 0 else CAP
    return [flat[:, i : i + chunk] for i in range(0, owners * CAP, chunk)]


def inject_kernel(steps, table_count, table_rows, with_halo, here_ref, *refs):
    table_refs, out_refs = refs[:table_count], refs[table_count:]
    rows, lanes = out_refs[0].shape
    here = here_ref[0].astype(jnp.float32)
    left, right = [], []
    for table_ref in table_refs:
        table = table_ref[table_ref.shape[0] - table_rows :]
        count = table.shape[1]
        slab = table[0:1]
        cell = table[1:2].astype(jnp.int32)
        row, lane = cell // lanes, cell % lanes
        in_lane = lax.broadcasted_iota(jnp.int32, (lanes, count), 0) == lane
        spread = jnp.where(in_lane, 1.0, 0.0).astype(jnp.bfloat16)
        each_row = lax.broadcasted_iota(jnp.int32, (rows, count), 0)
        in_row = [each_row == jnp.where(slab == here, row, -1)]
        if with_halo:
            in_row.append(each_row == jnp.where(slab == here - 1.0, row, -1))
            in_row.append(each_row == jnp.where(slab == here + 1.0, row, -1))
        rest = [table[2 + step : 3 + step] for step in range(steps)]
        for _ in range(PIECES):
            part = [r.astype(jnp.bfloat16).astype(jnp.float32) for r in rest]
            rest = [r - p for r, p in zip(rest, part)]
            picks = [(in_row[0], p) for p in part] + [(m, part[0]) for m in in_row[1:]]
            left.append(
                jnp.concatenate(
                    [jnp.where(m, p, 0.0).astype(jnp.bfloat16) for m, p in picks], axis=0
                )
            )
            right.append(spread)
    total = lax.dot_general(
        jnp.concatenate(left, axis=1),
        jnp.concatenate(right, axis=1),
        (((1,), (1,)), ((), ())),
        preferred_element_type=jnp.float32,
    )
    for i, out_ref in enumerate(out_refs):
        out_ref[...] = total[i * rows : (i + 1) * rows]


def injection(here, tables, steps, shape, with_halo):
    count = steps + 2 * with_halo
    entries = sum(t.shape[1] for t in tables)
    return on_chip(
        functools.partial(inject_kernel, steps, len(tables), tables[0].shape[0], with_halo),
        [(shape, jnp.float32)] * count,
        here,
        *tables,
        flops=EFFORT * 2 * PIECES * count * shape[0] * shape[1] * entries,
    )


def plane_stencil(plane):
    cells_y, lanes = plane.shape
    at_y = lax.broadcasted_iota(jnp.int32, plane.shape, 0)
    at_z = lax.broadcasted_iota(jnp.int32, plane.shape, 1)
    total = 3.0 * COEFFS[0] * plane
    for k in range(1, REACH + 1):
        pairs = (
            jnp.where(at_y >= k, pltpu.roll(plane, k, 0), 0.0)
            + jnp.where(at_y < cells_y - k, pltpu.roll(plane, cells_y - k, 0), 0.0)
            + jnp.where(at_z >= k, pltpu.roll(plane, k, 1), 0.0)
            + jnp.where(at_z < lanes - k, pltpu.roll(plane, lanes - k, 1), 0.0)
        )
        total = total + COEFFS[k] * pairs
    return total


def own_part(current, p, later, courant):
    total = plane_stencil(current[p])
    for k in range(1, REACH + 1):
        for q in (p - k, p + k):
            if 0 <= q < len(current):
                total = total + COEFFS[k] * current[q]
    return 2.0 * current[p] - later + courant * courant * total


def first_kernel(carry, *refs):
    now_hbm, later_hbm, courant_hbm, dest_hbm, cell_hbm, vals_hbm = refs[:6]
    later_ref, table_ref, now_ref, courant_ref = refs[6:10]
    dest_ref, cell_ref, vals_ref, sems = refs[-4:]
    pairs = [
        (dest_hbm, dest_ref),
        (cell_hbm, cell_ref),
        (vals_hbm, vals_ref),
        (now_hbm, now_ref),
        (later_hbm, later_ref),
        (courant_hbm, courant_ref),
    ]
    copies = [pltpu.make_async_copy(a, b, sems.at[i]) for i, (a, b) in enumerate(pairs)]
    for copy in copies:
        copy.start()
    for copy in copies[:3]:
        copy.wait()
    table_ref[...] = jnp.zeros_like(table_ref)
    table_ref[0:1] = dest_ref[...].astype(jnp.float32)
    table_ref[1:2] = cell_ref[...].astype(jnp.float32)
    table_ref[2 : 2 + vals_ref.shape[0]] = vals_ref[...]
    for copy in copies[3:6]:
        copy.wait()
    if carry:
        message_ref = refs[10]
        message_ref[0 : now_ref.shape[0]] = now_ref[...]
        message_ref[now_ref.shape[0] :] = table_ref[...]


def start_kernel(planes, now_ref, later_ref, courant_ref, part_ref):
    cells_y = now_ref.shape[0] // planes
    at = [slice(p * cells_y, (p + 1) * cells_y) for p in range(planes)]
    current = [now_ref[s] for s in at]
    for p, s in enumerate(at):
        part_ref[s] = own_part(current, p, later_ref[s], courant_ref[s])


def own_kernel(planes, step, fix_inject, last, *refs):
    refs = list(refs)
    current_ref, later_ref, courant_ref, fwd_ref, inject_ref = refs[:5]
    refs = refs[5:]
    fix_ref = refs.pop(0) if fix_inject else None
    grad_in_ref = refs.pop(0) if step > 1 else None
    part_ref = refs.pop(0)
    grad_ref = refs.pop(0)
    fixed_ref = refs.pop(0) if fix_inject else None
    weight_ref = refs.pop(0) if last else None
    cells_y = current_ref.shape[0] // planes
    at = [slice(p * cells_y, (p + 1) * cells_y) for p in range(planes)]
    current = [current_ref[s] for s in at]
    if fix_inject:
        current = [c + fix_ref[s] for c, s in zip(current, at)]
        for c, s in zip(current, at):
            fixed_ref[s] = c
    for p, s in enumerate(at):
        courant = courant_ref[s]
        part_ref[s] = own_part(current, p, later_ref[s], courant) + inject_ref[s]
        grad = fwd_ref[step - 1, s].astype(jnp.float32) * current[p]
        if step > 1:
            grad = grad + grad_in_ref[s]
        if last:
            inverse = 1.0 / courant
            grad = grad * inverse
            weight_ref[s] = fwd_ref[step, s].astype(jnp.float32) * inverse
        grad_ref[s] = grad


def halo_kernel(planes, slabs, fix_inject, last, here_ref, *refs):
    refs = list(refs)
    inner_ref, outer_ref, part_ref, courant_ref = refs[:4]
    refs = refs[4:]
    fix_refs = (refs.pop(0), refs.pop(0)) if fix_inject else None
    weight_ref, grad_in_ref = (refs.pop(0), refs.pop(0)) if last else (None, None)
    fresh_ref = refs.pop(0)
    grad_ref = refs.pop(0) if last else None
    here = here_ref[0]
    even = here % 2 == 0
    rows = part_ref.shape[0]
    cells_y = rows // planes
    at = [slice(p * cells_y, (p + 1) * cells_y) for p in range(planes)]
    low, high = {}, {}
    for p in range(planes - REACH, planes):
        plane = jnp.where(even, outer_ref[at[p]], inner_ref[at[p]])
        if fix_inject:
            plane = plane + fix_refs[0][at[p]]
        low[p - planes] = jnp.where(here == 0, 0.0, plane)
    for p in range(REACH):
        plane = jnp.where(even, inner_ref[at[p]], outer_ref[at[p]])
        if fix_inject:
            plane = plane + fix_refs[1][at[p]]
        high[p + planes] = jnp.where(here == slabs - 1, 0.0, plane)
    for p, s in enumerate(at):
        terms = []
        for k in range(1, REACH + 1):
            if p - k < 0:
                terms.append(COEFFS[k] * low[p - k])
            if p + k >= planes:
                terms.append(COEFFS[k] * high[p + k])
        courant = courant_ref[s]
        fresh = part_ref[s] + courant * courant * sum(terms[1:], terms[0])
        fresh_ref[s] = fresh
        if last:
            grad_ref[s] = grad_in_ref[s] + weight_ref[s] * fresh


def sum_over(value, axis):
    count = lax.axis_size(axis)
    if count & (count - 1):
        return lax.psum(value, axis)
    distance = count // 2
    while distance:
        value = value + lax.ppermute(value, axis, [(i, i ^ distance) for i in range(count)])
        distance //= 2
    return value


def on_device(adjoint_now, adjoint_later, courant, fwd_acc, surf_dest, surf_cell, surf_vals):
    planes, cells_y, lanes = courant.shape
    steps = fwd_acc.shape[1]
    rows = planes * cells_y
    shape = (rows, lanes)
    entries = surf_cell.shape[0]
    slabs = lax.axis_size("tgt")
    here = lax.axis_index("tgt").reshape(1)
    now = adjoint_now.reshape(shape)
    table_rows = -(-(2 + steps) // 8) * 8
    everywhere = (
        1 < slabs == slabs & -slabs and slabs * entries <= GATHER_LIMIT and entries == lanes
    )

    f32 = jnp.float32
    fwd = fwd_acc.reshape(steps, rows, lanes)
    later_here, table, current, courant_here, *message = on_chip(
        functools.partial(first_kernel, everywhere),
        [
            (shape, f32),
            ((table_rows, entries), f32),
            (shape, f32),
            (shape, f32),
        ]
        + [((rows + table_rows, lanes), f32)] * everywhere,
        now,
        adjoint_later.reshape(shape),
        courant.reshape(shape),
        surf_dest.reshape(1, entries),
        surf_cell.reshape(1, entries),
        surf_vals.reshape(steps, entries),
        flops=40 * rows * lanes,
        scratch=[
            pltpu.VMEM((1, entries), surf_dest.dtype),
            pltpu.VMEM((1, entries), surf_cell.dtype),
            pltpu.VMEM((steps, entries), f32),
            pltpu.SemaphoreType.DMA((6,)),
        ],
        in_hbm=range(6),
    )
    received = exchange(*message, current) if everywhere else exchange(current)
    (part,) = on_chip(
        functools.partial(start_kernel, planes),
        [(shape, f32)],
        current,
        later_here,
        courant_here,
        flops=40 * rows * lanes,
    )
    if everywhere:
        tables = [table, received[0]] + [
            lax.ppermute(table, "tgt", [(i, i ^ far) for i in range(slabs)])
            for far in range(slabs - 1, 1, -1)
        ]
        inject = None
    else:
        tables = slotted_tables(table, surf_dest, slabs)
        inject = injection(here, tables, steps, shape, False)
        part = part + inject[0]

    fixes, extra, later_field, grad = [], [], None, None
    for step in range(steps):
        last = step == steps - 1
        fix = everywhere and step == 1
        if step:
            outs = [(shape, f32)] * (2 + fix + last)
            args = [current, later_field, courant_here, fwd, inject[step]]
            args += [inject[0]] if fix else []
            args += [grad] if step > 1 else []
            part, grad, *extra = on_chip(
                functools.partial(own_kernel, planes, step, fix, last),
                outs,
                *args,
                flops=40 * rows * lanes,
            )
            if fix:
                current = extra.pop(0)
        args = [here, *received, part, courant_here, *fixes]
        args += [*extra, grad] if last else []
        fresh, *other = on_chip(
            functools.partial(halo_kernel, planes, slabs, fix, last),
            [(shape, f32)] * (1 + last),
            *args,
            flops=10 * rows * lanes,
        )
        later_field, current, fixes = current, fresh, []
        if not last:
            received = exchange(fresh)
        if everywhere and step == 0:
            inject = injection(here, tables, steps, shape, True)
            fixes = inject[steps:]
    grad = sum_over(other[0], "shot")
    return (current.reshape(adjoint_now.shape), grad.reshape(courant.shape))


def solution(mesh):
    in_specs = (
        P(("grp", "shot"), "tgt", None, None),
        P(("grp", "shot"), "tgt", None, None),
        P("tgt", None, None),
        P(("grp", "shot"), None, "tgt", None, None),
        P("tgt", None),
        P("tgt"),
        P(("grp", "shot"), None, "tgt"),
    )
    out_specs = (P(("grp", "shot"), "tgt", None, None), P(("grp", "tgt"), None, None))
    return jax.shard_map(
        on_device, mesh=mesh, in_specs=in_specs, out_specs=out_specs, check_vma=False
    )
```
